512 devices in a mesh: ta: 8 (over z), af: 8 (over y_lo, x), sa: 8 (over y_hi, core).
Axes of the slice: x: 4, y: 8 (y_hi: 4, y_lo: 2; y = y_hi * 2 + y_lo), z: 8, core: 2. Of those that a mesh axis runs over, the one named last changes fastest.
Arguments:
- blocks: bfloat16 [8, 8, 8, 4, 64, 4096], P('ta', 'af', 'sa'), may hold values from -6 to 6
- coords: int32 [8, 8, 8, 4, 3], P('ta', 'af', 'sa'), may hold values from 0 to 1, as said below
- counts: int32 [8, 8, 8], P('ta', 'af', 'sa'), may hold values from 1 to 4, as said below
- time_factor: float32 [8, 128, 256], P('ta', ('af', 'sa')), may hold values from -2.4 to 2.4
- freq_factor: float32 [8, 128, 256], P('af', ('ta', 'sa')), may hold values from -2.4 to 2.4
- subj_factor: float32 [8, 128, 256], P('sa', ('ta', 'af')), may hold values from -2.4 to 2.4
- time_velocity: float32 [8, 128, 256], P('ta', ('af', 'sa')), may hold values from -1.8 to 1.8
- freq_velocity: float32 [8, 128, 256], P('af', ('ta', 'sa')), may hold values from -1.8 to 1.8
- subj_velocity: float32 [8, 128, 256], P('sa', ('ta', 'af')), may hold values from -1.8 to 1.8
Outputs:
- new_time: float32 [8, 128, 256], P('ta', ('af', 'sa'))
- new_freq: float32 [8, 128, 256], P('af', ('ta', 'sa'))
- new_subj: float32 [8, 128, 256], P('sa', ('ta', 'af'))
- new_time_velocity: float32 [8, 128, 256], P('ta', ('af', 'sa'))
- new_freq_velocity: float32 [8, 128, 256], P('af', ('ta', 'sa'))
- new_subj_velocity: float32 [8, 128, 256], P('sa', ('ta', 'af'))
The draws below stay inside these ranges and needn't reach their ends.
Inputs may be any that keep to these rules, and one draw needn't show every extreme that they name: `coords`: entries are 0 or 1; the 4 slots of a device name distinct positions. `counts`: some device has 4 filled slots and some has 1.
All inputs are finite; a program needn't handle non-finite values.
Results may differ from the reference program's by a relative error of at most 0.005.
Values may be sent and summed in bfloat16 or wider, within the bound.
No kernel may reach another device: no remote copies, remote signals or barrier semaphores. Data moves between devices by JAX's collectives and lax.ppermute only.
A program may use at most 64 MiB of HBM per device.

```python
import jax
import jax.numpy as jnp
from jax import lax

R = 256
BT = 64
BF = 64
BS = 64
CAP = 4
N_TA = 8
N_AF = 8
N_SA = 8


def draw_coords(key, part):
    total = N_TA * N_AF * N_SA
    keys = jax.random.split(jax.random.fold_in(key, 11), total)
    chosen = jax.vmap(lambda single: jax.random.permutation(single, 8))(keys)[:, :CAP]
    stacked = jnp.stack([chosen // 4, chosen // 2 % 2, chosen % 2], axis=-1)
    return stacked.reshape(N_TA, N_AF, N_SA, CAP, 3).astype(jnp.int32)


def draw_counts(key, part):
    total = N_TA * N_AF * N_SA
    filled = jax.random.randint(jax.random.fold_in(key, 5), (total,), 1, CAP + 1)
    highest = jax.random.randint(jax.random.fold_in(key, 6), (), 0, total)
    lowest = (highest + 1 + jax.random.randint(jax.random.fold_in(key, 7), (), 0, total - 1)) % total
    filled = filled.at[highest].set(CAP).at[lowest].set(1)
    return filled.reshape(N_TA, N_AF, N_SA).astype(jnp.int32)


def level_of(rng, shape, pieces, least, top_value):
    gain = 1.0
    for dim, parts in pieces:
        draws = jax.random.uniform(jax.random.fold_in(jax.random.fold_in(rng, 6), dim), (parts,), jnp.float32, least / len(pieces), top_value / len(pieces))
        gain = gain * jnp.repeat(jnp.exp(draws), shape[dim] // parts).reshape((-1,) + (1,) * (len(shape) - 1 - dim))
    return gain


def centred(stream_key, shape, spread, bound, cuts=(), kind=jnp.bfloat16):
    array = spread * jax.random.normal(stream_key, shape, jnp.float32)
    if cuts:
        array = array * level_of(stream_key, shape, cuts, -0.22, 0.18)
    return jnp.clip(array, -bound, bound).astype(kind)


def setup_inputs(seed: int = 0) -> dict:
    key_list = jax.random.split(jax.random.key(seed), 10)
    return {
        "blocks": centred(key_list[0], (N_TA, N_AF, N_SA, CAP, BT, BF * BS), 1.0, 6.0, ((0, 8), (1, 8), (2, 8))),
        "coords": draw_coords(jax.random.fold_in(key_list[9], 71), 0),
        "counts": draw_counts(jax.random.fold_in(key_list[9], 71), 0),
        "time_factor": centred(key_list[3], (N_TA, 2 * BT, R), 0.4, 2.4, ((0, 8), (1, 64)), jnp.float32),
        "freq_factor": centred(key_list[4], (N_AF, 2 * BF, R), 0.4, 2.4, ((0, 8), (1, 64)), jnp.float32),
        "subj_factor": centred(key_list[5], (N_SA, 2 * BS, R), 0.4, 2.4, ((0, 8), (1, 64)), jnp.float32),
        "time_velocity": centred(key_list[6], (N_TA, 2 * BT, R), 0.3, 1.8, ((0, 8), (1, 64)), jnp.float32),
        "freq_velocity": centred(key_list[7], (N_AF, 2 * BF, R), 0.3, 1.8, ((0, 8), (1, 64)), jnp.float32),
        "subj_velocity": centred(key_list[8], (N_SA, 2 * BS, R), 0.3, 1.8, ((0, 8), (1, 64)), jnp.float32),
    }


def block_terms(block_data, time_table, freq_table, subj_table, position, valid, freq_extent, subj_extent):
    time_extent = block_data.shape[0]
    time_block = lax.dynamic_slice_in_dim(time_table, position[0] * time_extent, time_extent, 0)
    freq_block = lax.dynamic_slice_in_dim(freq_table, position[1] * freq_extent, freq_extent, 0)
    subj_block = lax.dynamic_slice_in_dim(subj_table, position[2] * subj_extent, subj_extent, 0)
    freq_wide = freq_block.astype(jnp.float32)
    subj_wide = subj_block.astype(jnp.float32)
    khatri = (freq_wide[:, None, :] * subj_wide[None, :, :]).astype(jnp.bfloat16)
    khatri = khatri.reshape(freq_extent * subj_extent, -1)
    approx = lax.dot_general(time_block, khatri, (((1,), (1,)), ((), ())), preferred_element_type=jnp.float32)
    observed = block_data.astype(jnp.float32)
    misfit = ((approx - observed) * valid).astype(jnp.bfloat16)
    grad_time = jnp.dot(misfit, khatri, preferred_element_type=jnp.float32)
    contracted = lax.dot_general(misfit, time_block, (((0,), (0,)), ((), ())), preferred_element_type=jnp.float32)
    contracted = contracted.reshape(freq_extent, subj_extent, -1)
    grad_freq = jnp.sum(contracted * subj_wide[None, :, :], axis=1)
    grad_subj = jnp.sum(contracted * freq_wide[:, None, :], axis=0)
    return grad_time, grad_freq, grad_subj


def add_block(accumulated, block_grad, group, offset):
    corner = (group, offset, jnp.zeros((), jnp.int32))
    current = lax.dynamic_slice(accumulated, corner, (1, block_grad.shape[0], block_grad.shape[1]))
    return lax.dynamic_update_slice(accumulated, current + block_grad[None], corner)


def reference(blocks, coords, counts, time_factor, freq_factor, subj_factor, time_velocity, freq_velocity, subj_velocity):
    time_table = time_factor.astype(jnp.bfloat16)
    freq_table = freq_factor.astype(jnp.bfloat16)
    subj_table = subj_factor.astype(jnp.bfloat16)
    slots = N_TA * N_AF * N_SA * CAP
    flat_blocks = blocks.reshape(slots, BT, BF * BS)
    flat_coords = coords.reshape(slots, 3).astype(jnp.int32)
    serial = jnp.arange(slots, dtype=jnp.int32)
    device = serial // CAP
    slot_index = serial % CAP
    group_s = device % N_SA
    group_a = (device // N_SA) % N_AF
    group_t = device // (N_SA * N_AF)
    occupied = slot_index < counts.reshape(-1).astype(jnp.int32)[device]

    def visit_slot(running, slot_data):
        block_data, position, group_time, group_freq, group_subj, alive = slot_data

        def compute():
            return block_terms(block_data, time_table[group_time], freq_table[group_freq], subj_table[group_subj], position, jnp.ones((), jnp.float32), BF, BS)

        def skip():
            return (jnp.zeros((BT, R), jnp.float32), jnp.zeros((BF, R), jnp.float32), jnp.zeros((BS, R), jnp.float32))

        grad_time, grad_freq, grad_subj = lax.cond(alive, compute, skip)
        return (add_block(running[0], grad_time, group_time, position[0] * BT),
                add_block(running[1], grad_freq, group_freq, position[1] * BF),
                add_block(running[2], grad_subj, group_subj, position[2] * BS)), None

    initial = (jnp.zeros(time_factor.shape, jnp.float32), jnp.zeros(freq_factor.shape, jnp.float32), jnp.zeros(subj_factor.shape, jnp.float32))
    gradients, unused = lax.scan(visit_slot, initial, (flat_blocks, flat_coords, group_t, group_a, group_s, occupied))
    new_time_velocity = 0.9 * time_velocity + gradients[0] / 64.0
    new_freq_velocity = 0.9 * freq_velocity + gradients[1] / 64.0
    new_subj_velocity = 0.9 * subj_velocity + gradients[2] / 64.0
    new_time = time_factor - 0.5 * new_time_velocity
    new_freq = freq_factor - 0.5 * new_freq_velocity
    new_subj = subj_factor - 0.5 * new_subj_velocity
    return (new_time, new_freq, new_subj, new_time_velocity, new_freq_velocity, new_subj_velocity)
```

```python
import functools

import jax
import jax.numpy as jnp
from jax import lax
from jax.experimental import pallas as pl
from jax.experimental.pallas import tpu as pltpu
from jax.sharding import PartitionSpec as P

BF16 = jnp.bfloat16
F32 = jnp.float32
ROWS = 2
HALF = 128
SEND = BF16


def put_rows(tile, at, rows):
    tile[at : at + 2, :] = rows[:, :HALF]
    tile[at + 2 : at + 4, :] = rows[:, HALF:]


def pack_factors(n_af, n_sa, time_ref, freq_ref, subj_ref, out_ref, with_freq, with_subj):
    mine = lax.axis_index("af")
    put_rows(with_freq, 0, time_ref[0])
    put_rows(with_subj, 0, time_ref[0])
    put_rows(with_freq, 4, freq_ref[0])
    put_rows(with_subj, 4, subj_ref[0])
    freq_tile = with_freq[...].astype(BF16)
    subj_tile = with_subj[...].astype(BF16)
    out_ref[...] = jnp.broadcast_to(subj_tile[None], out_ref.shape)
    out_ref[pl.ds(mine * n_sa, n_sa)] = jnp.broadcast_to(freq_tile[None], (n_sa, 8, HALF))


def join_factors(n_af, n_sa, got_ref, subj_ref, out_ref, wide, joined):
    af = lax.axis_index("af")
    sa = lax.axis_index("sa")
    slots = n_af * n_sa
    wide[...] = got_ref[...].astype(F32).reshape(slots * 8, HALF)
    own = subj_ref[0].astype(BF16).astype(F32)
    is_own = lax.broadcasted_iota(jnp.int32, (n_af, HALF), 0) == af
    for half in range(2):
        for row in range(ROWS):
            at = 4 + 2 * half + row
            freq = wide[pl.ds(af * (n_sa * 8) + at, n_sa, stride=8), :]
            joined[half, pl.ds(row, n_sa, stride=ROWS), :] = freq
            subj = wide[pl.ds(sa * 8 + at, n_af, stride=n_sa * 8), :]
            mine = own[row : row + 1, half * HALF : (half + 1) * HALF]
            subj = jnp.where(is_own, mine, subj)
            joined[half, pl.ds(ROWS * n_sa + row, n_af, stride=ROWS), :] = subj
    rows = jnp.concatenate([joined[0], joined[1]], axis=1).astype(BF16)
    for peer in range(out_ref.shape[0]):
        out_ref[peer] = rows


def main_body(
    dims,
    coords_ref,
    counts_ref,
    blocks_ref,
    first_ref,
    second_ref,
    pair_ref,
    time_ref,
    wide,
    time_table,
    acc_time,
    acc_freq,
    acc_subj,
):
    n_ta, n_af, n_sa, bt, bf, bs, step = dims
    slot = pl.program_id(0)
    slots = n_af * n_sa

    @pl.when(slot == 0)
    def _():
        wide[...] = first_ref[...].astype(F32).reshape(slots * 8, HALF)
        for half in range(2):
            for row in range(ROWS):
                time_table[half, pl.ds(row, slots, stride=ROWS), :] = wide[
                    pl.ds(2 * half + row, slots, stride=8), :
                ]
        acc_time[...] = jnp.zeros_like(acc_time)
        acc_freq[...] = jnp.zeros_like(acc_freq)
        acc_subj[...] = jnp.zeros_like(acc_subj)

    @pl.when(slot < counts_ref[0, 0, 0])
    def _():
        time_at = pl.multiple_of(coords_ref[0, 0, 0, slot, 0] * bt, bt)
        freq_at = coords_ref[0, 0, 0, slot, 1]
        subj_at = coords_ref[0, 0, 0, slot, 2]
        half_ta = n_ta // 2
        n_freq = ROWS * n_sa
        a = jnp.concatenate(
            [time_table[half, pl.ds(time_at, bt), :].astype(BF16) for half in range(2)], axis=1
        )
        b = second_ref[pl.ds(freq_at * half_ta, half_ta), :n_freq, :].reshape(bf, -1).astype(F32)
        c = second_ref[pl.ds(subj_at * half_ta, half_ta), n_freq:, :].reshape(bs, -1).astype(F32)
        freq_row = pl.multiple_of(freq_at * bf, bf)
        subj_row = pl.multiple_of(subj_at * bs, bs)
        grad_time = jnp.zeros(a.shape, F32)
        grad_subj = jnp.zeros(c.shape, F32)
        for j in range(0, bf, step):
            khatri = (b[j : j + step][:, None, :] * c[None]).astype(BF16).reshape(step * bs, -1)
            approx = lax.dot_general(
                a, khatri, (((1,), (1,)), ((), ())), preferred_element_type=F32
            )
            observed = blocks_ref[0, 0, 0, 0, :, j * bs : (j + step) * bs].astype(F32)
            misfit = (approx - observed).astype(BF16)
            grad_time += jnp.dot(misfit, khatri, preferred_element_type=F32)
            contracted = lax.dot_general(
                misfit, a, (((0,), (0,)), ((), ())), preferred_element_type=F32
            ).reshape(step, bs, -1)
            acc_freq[pl.ds(freq_row + j, step), :] += jnp.sum(contracted * c[None], axis=1)
            for k in range(step):
                grad_subj += contracted[k] * b[j + k : j + k + 1]
        acc_time[pl.ds(time_at, bt), :] += grad_time
        acc_subj[pl.ds(subj_row, bs), :] += grad_subj

    @pl.when(slot == pl.num_programs(0) - 1)
    def _():
        for half in range(2):
            time_ref[half] = acc_time[:, half * HALF : (half + 1) * HALF]
        for t in range(n_ta):
            n_freq, n_subj = ROWS * n_sa, ROWS * n_af
            pair_ref[t, :n_freq, :] = acc_freq[t * n_freq : (t + 1) * n_freq, :].astype(SEND)
            pair_ref[t, n_freq:, :] = acc_subj[t * n_subj : (t + 1) * n_subj, :].astype(SEND)


def pack_grads(n_af, n_sa, got_ref, time_ref, out_ref, own_ref, summed, wide):
    af = lax.axis_index("af")
    slots = n_af * n_sa
    n_freq = ROWS * n_sa
    total = jnp.sum(got_ref[...].astype(F32), axis=0)
    for half in range(2):
        summed[half] = total[:, half * HALF : (half + 1) * HALF]
    for half in range(2):
        for row in range(ROWS):
            wide[pl.ds(2 * half + row, slots, stride=8), :] = time_ref[
                half, pl.ds(row, slots, stride=ROWS), :
            ]
            at = 4 + 2 * half + row
            for peer in range(n_af):
                there = n_freq + ROWS * peer + row
                subj = summed[half, there : there + 1, :]
                wide[pl.ds(peer * n_sa * 8 + at, n_sa, stride=8), :] = jnp.broadcast_to(
                    subj, (n_sa, HALF)
                )
            wide[pl.ds(af * (n_sa * 8) + at, n_sa, stride=8), :] = summed[
                half, pl.ds(row, n_sa, stride=ROWS), :
            ]
        own_ref[:, half * HALF : (half + 1) * HALF] = summed[
            half, pl.ds(n_freq + ROWS * af, ROWS), :
        ]
    out_ref[...] = wide[...].astype(SEND).reshape(slots, 8, HALF)


def update(
    n_af,
    n_sa,
    got_ref,
    own_ref,
    time_ref,
    freq_ref,
    subj_ref,
    time_vel_ref,
    freq_vel_ref,
    subj_vel_ref,
    new_time_ref,
    new_freq_ref,
    new_subj_ref,
    new_time_vel_ref,
    new_freq_vel_ref,
    new_subj_vel_ref,
):
    af = lax.axis_index("af")
    sa = lax.axis_index("sa")
    time = jnp.sum(got_ref[...].astype(F32), axis=0)
    freq = jnp.sum(got_ref[pl.ds(af * n_sa, n_sa)].astype(F32), axis=0)
    subj = jnp.zeros_like(freq)
    for peer in range(n_af):
        there = got_ref[peer * n_sa + sa].astype(F32)
        subj += jnp.where(peer == af, jnp.zeros_like(there), there)
    own = own_ref[...]
    for half in range(2):
        lanes = slice(half * HALF, (half + 1) * HALF)
        rows = slice(2 * half, 2 * half + 2)
        more = slice(4 + 2 * half, 6 + 2 * half)
        for grad, old, vel, new, new_vel in (
            (time[rows], time_ref, time_vel_ref, new_time_ref, new_time_vel_ref),
            (freq[more], freq_ref, freq_vel_ref, new_freq_ref, new_freq_vel_ref),
            (subj[more] + own[:, lanes], subj_ref, subj_vel_ref, new_subj_ref, new_subj_vel_ref),
        ):
            velocity = 0.9 * vel[0, :, lanes] + grad / 64.0
            new_vel[0, :, lanes] = velocity
            new[0, :, lanes] = old[0, :, lanes] - 0.5 * velocity


def per_device(sizes, *args):
    n_ta, n_af, n_sa = sizes
    blocks, coords, counts, time, freq, subj, time_vel, freq_vel, subj_vel = args
    slots = n_af * n_sa
    cap, bt = blocks.shape[3:5]
    rank = time.shape[-1]
    bf = ROWS * n_ta * n_sa // 2
    bs = ROWS * n_ta * n_af // 2
    pair_rows = ROWS * (n_sa + n_af)
    tile = jax.ShapeDtypeStruct((slots, 8, HALF), BF16)

    packed = pl.pallas_call(
        functools.partial(pack_factors, n_af, n_sa),
        out_shape=tile,
        scratch_shapes=[pltpu.VMEM((8, HALF), F32)] * 2,
        name="pack_factors",
    )(time, freq, subj)
    first = lax.all_to_all(packed, ("af", "sa"), 0, 0, tiled=True)
    joined = pl.pallas_call(
        functools.partial(join_factors, n_af, n_sa),
        out_shape=jax.ShapeDtypeStruct((n_ta, pair_rows, rank), BF16),
        scratch_shapes=[pltpu.VMEM((slots * 8, HALF), F32), pltpu.VMEM((2, pair_rows, HALF), F32)],
        name="join_factors",
    )(first, subj)
    second = lax.all_to_all(joined, "ta", 0, 0, tiled=True)

    table = (ROWS * slots, rank)
    halves = (2, ROWS * slots, HALF)
    step = min(8, bf)
    dims = (n_ta, n_af, n_sa, bt, bf, bs, step)
    pair, time_grad = pl.pallas_call(
        functools.partial(main_body, dims),
        grid=(cap,),
        in_specs=[
            pl.BlockSpec(memory_space=pltpu.SMEM),
            pl.BlockSpec(memory_space=pltpu.SMEM),
            pl.BlockSpec((1, 1, 1, 1, bt, bf * bs), lambda i: (0, 0, 0, i, 0, 0)),
            pl.BlockSpec((slots, 8, HALF), lambda i: (0, 0, 0)),
            pl.BlockSpec((n_ta, pair_rows, rank), lambda i: (0, 0, 0)),
        ],
        out_specs=[
            pl.BlockSpec((n_ta, pair_rows, rank), lambda i: (0, 0, 0)),
            pl.BlockSpec(halves, lambda i: (0, 0, 0)),
        ],
        out_shape=[
            jax.ShapeDtypeStruct((n_ta, pair_rows, rank), SEND),
            jax.ShapeDtypeStruct(halves, F32),
        ],
        scratch_shapes=[
            pltpu.VMEM((slots * 8, HALF), F32),
            pltpu.VMEM(halves, F32),
            pltpu.VMEM(table, F32),
            pltpu.VMEM((2 * bf, rank), F32),
            pltpu.VMEM((2 * bs, rank), F32),
        ],
        compiler_params=pltpu.CompilerParams(
            dimension_semantics=("arbitrary",), vmem_limit_bytes=32 << 20
        ),
        name="block_grads",
    )(coords, counts, blocks, first, second)

    third = lax.all_to_all(pair, "ta", 0, 0, tiled=True)
    packed_grads, own = pl.pallas_call(
        functools.partial(pack_grads, n_af, n_sa),
        out_shape=[
            jax.ShapeDtypeStruct((slots, 8, HALF), SEND),
            jax.ShapeDtypeStruct((ROWS, rank), F32),
        ],
        scratch_shapes=[
            pltpu.VMEM((2, pair_rows, HALF), F32),
            pltpu.VMEM((slots * 8, HALF), F32),
        ],
        name="pack_grads",
    )(third, time_grad)
    fourth = lax.all_to_all(packed_grads, ("af", "sa"), 0, 0, tiled=True)
    return pl.pallas_call(
        functools.partial(update, n_af, n_sa),
        out_shape=[jax.ShapeDtypeStruct(time.shape, F32)] * 6,
        name="update",
    )(fourth, own, time, freq, subj, time_vel, freq_vel, subj_vel)


def solution(mesh):
    sizes = tuple(mesh.shape[name] for name in ("ta", "af", "sa"))
    factors = (P("ta", ("af", "sa"), None), P("af", ("ta", "sa"), None), P("sa", ("ta", "af"), None))
    return jax.shard_map(
        lambda *args: tuple(per_device(sizes, *args)),
        mesh=mesh,
        in_specs=(
            P("ta", "af", "sa", None, None, None),
            P("ta", "af", "sa", None, None),
            P("ta", "af", "sa"),
            *factors,
            *factors,
        ),
        out_specs=(*factors, *factors),
        check_vma=False,
    )
```

```python
import functools

import jax
import jax.numpy as jnp
from jax import lax
from jax.experimental import pallas as pl
from jax.experimental.pallas import tpu as pltpu
from jax.sharding import PartitionSpec as P

BF16 = jnp.bfloat16
F32 = jnp.float32
ROWS = 2
HALF = 128
BIG = 56 * 1000 * 1000
SMALL = 4 << 20
SEND = BF16


def put_rows(tile, at, rows):
    tile[at : at + 2, :] = rows[:, :HALF]
    tile[at + 2 : at + 4, :] = rows[:, HALF:]


def pack_factors(n_sa, own_ref, out_ref, with_freq, with_subj):
    mine = lax.axis_index("af")
    put_rows(with_freq, 0, own_ref[0])
    put_rows(with_subj, 0, own_ref[0])
    put_rows(with_freq, 4, own_ref[1])
    put_rows(with_subj, 4, own_ref[2])
    freq_tile = with_freq[...].astype(BF16)
    subj_tile = with_subj[...].astype(BF16)
    out_ref[...] = jnp.broadcast_to(subj_tile[None], out_ref.shape)
    out_ref[pl.ds(mine * n_sa, n_sa)] = jnp.broadcast_to(freq_tile[None], (n_sa, 8, HALF))


def join_factors(n_af, n_sa, got_ref, packed_ref, out_ref, time_ref, wide, joined, time_table):
    af = lax.axis_index("af")
    sa = lax.axis_index("sa")
    slots = n_af * n_sa
    wide[...] = got_ref[...].astype(F32).reshape(slots * 8, HALF)
    own = packed_ref[jnp.where(af == 0, n_sa, 0)].astype(F32)
    is_own = lax.broadcasted_iota(jnp.int32, (n_af, HALF), 0) == af
    for half in range(2):
        for row in range(ROWS):
            at = 4 + 2 * half + row
            freq = wide[pl.ds(af * (n_sa * 8) + at, n_sa, stride=8), :]
            joined[half, pl.ds(row, n_sa, stride=ROWS), :] = freq
            subj = wide[pl.ds(sa * 8 + at, n_af, stride=n_sa * 8), :]
            subj = jnp.where(is_own, own[at : at + 1], subj)
            joined[half, pl.ds(ROWS * n_sa + row, n_af, stride=ROWS), :] = subj
    rows = jnp.concatenate([joined[0], joined[1]], axis=1).astype(BF16)
    for peer in range(out_ref.shape[0]):
        out_ref[peer] = rows
    for half in range(2):
        for row in range(ROWS):
            time_table[half, pl.ds(row, slots, stride=ROWS), :] = wide[
                pl.ds(2 * half + row, slots, stride=8), :
            ]
    time_ref[...] = jnp.concatenate([time_table[0], time_table[1]], axis=1).astype(BF16)


def dot(a, b, contract=((1,), (0,))):
    return lax.dot_general(a, b, (contract, ((), ())), preferred_element_type=F32)


def gram(table):
    return dot(table, table, ((0,), (0,)))


def model_part(rows, grams):
    high = grams.astype(BF16)
    low = (grams - high.astype(F32)).astype(BF16)
    return dot(rows, high) + dot(rows, low)


def take(ref, which, extent):
    return ref[pl.ds(pl.multiple_of(which * extent, extent), extent), :]


def pair_blocks(ref, freq_at, subj_at, n_freq):
    half_ta = ref.shape[0] // 2
    rank = ref.shape[2]
    freq = ref[pl.ds(freq_at * half_ta, half_ta), :n_freq, :]
    subj = ref[pl.ds(subj_at * half_ta, half_ta), n_freq:, :]
    return freq.reshape(-1, rank), subj.reshape(-1, rank)


def fetch_blocks(blocks_ref, data, sems):
    copies = [
        pltpu.make_async_copy(blocks_ref.at[0, 0, 0, slot], data.at[slot], sems.at[slot])
        for slot in range(data.shape[0])
    ]
    for copy in copies:
        copy.start()
    return copies


def pair_body(
    n_freq,
    where_ref,
    blocks_ref,
    time_ref,
    second_ref,
    pair_ref,
    data,
    grams,
    freq,
    subj,
    sems,
):
    copies = fetch_blocks(blocks_ref, data, sems)
    n_ta = second_ref.shape[0]
    bf = freq.shape[0] // 2
    bs = subj.shape[0] // 2
    bt = time_ref.shape[0] // 2
    n_subj = second_ref.shape[1] - n_freq
    freq[...] = jnp.zeros_like(freq)
    subj[...] = jnp.zeros_like(subj)
    for which in range(2):
        b, c = pair_blocks(second_ref, which, which, n_freq)
        grams[which] = gram(take(time_ref, which, bt))
        grams[2 + which] = gram(b)
        grams[4 + which] = gram(c)
    step = min(8, bf)
    for slot, copy in enumerate(copies):
        copy.wait()

        @pl.when(slot < where_ref[3, slot])
        def _(slot=slot):
            time_at = where_ref[0, slot]
            freq_at = where_ref[1, slot]
            subj_at = where_ref[2, slot]
            a = take(time_ref, time_at, bt)
            b, c = pair_blocks(second_ref, freq_at, subj_at, n_freq)
            time_gram = grams[time_at]
            freq_model = model_part(b, time_gram * grams[4 + subj_at])
            subj_model = model_part(c, time_gram * grams[2 + freq_at])
            wide_b, wide_c = b.astype(F32), c.astype(F32)
            freq_data = []
            subj_data = jnp.zeros(wide_c.shape, F32)
            for j in range(0, bf, step):
                cells = data[slot, :, j * bs : (j + step) * bs]
                cube = dot(cells, a, ((0,), (0,))).reshape(step, bs, -1)
                freq_data.append(jnp.sum(cube * wide_c[None], axis=1))
                for k in range(step):
                    subj_data += cube[k] * wide_b[j + k : j + k + 1]
            freq_data = jnp.concatenate(freq_data, axis=0)
            freq[pl.ds(pl.multiple_of(freq_at * bf, bf), bf), :] += freq_model - freq_data
            subj[pl.ds(pl.multiple_of(subj_at * bs, bs), bs), :] += subj_model - subj_data

    for t in range(n_ta):
        pair_ref[t, :n_freq, :] = freq[t * n_freq : (t + 1) * n_freq, :].astype(SEND)
        pair_ref[t, n_freq:, :] = subj[t * n_subj : (t + 1) * n_subj, :].astype(SEND)


def time_body(
    n_freq, where_ref, blocks_ref, time_ref, second_ref, out_ref, data, grad, sems
):
    copies = fetch_blocks(blocks_ref, data, sems)
    bt = data.shape[1]
    grad[...] = jnp.zeros_like(grad)
    for slot, copy in enumerate(copies):
        copy.wait()

        @pl.when(slot < where_ref[3, slot])
        def _(slot=slot):
            time_at = where_ref[0, slot]
            a = take(time_ref, time_at, bt)
            b, c = pair_blocks(
                second_ref, where_ref[1, slot], where_ref[2, slot], n_freq
            )
            bf, bs = b.shape[0], c.shape[0]
            total = model_part(a, gram(b) * gram(c))
            wide_b = b.astype(F32)
            zero = jnp.zeros_like(c)
            both = jnp.concatenate(
                [jnp.concatenate([c, zero], axis=1), jnp.concatenate([zero, c], axis=1)], axis=0
            )
            rank = c.shape[1]
            for j in range(0, bf, 2):
                part = dot(data[slot, :, j * bs : (j + 2) * bs], both)
                total -= part[:, :rank] * wide_b[j : j + 1]
                total -= part[:, rank:] * wide_b[j + 1 : j + 2]
            grad[pl.ds(pl.multiple_of(time_at * bt, bt), bt), :] += total

    for half in range(2):
        out_ref[half] = grad[:, half * HALF : (half + 1) * HALF]


def kernel_call(body, out_shape, in_spaces, scratch, name, cost, limit):
    return pl.pallas_call(
        body,
        out_shape=out_shape,
        in_specs=[pl.BlockSpec(memory_space=space) for space in in_spaces],
        out_specs=jax.tree.map(lambda _: pl.BlockSpec(memory_space=pltpu.VMEM), out_shape),
        scratch_shapes=scratch,
        compiler_params=pltpu.CompilerParams(vmem_limit_bytes=limit),
        cost_estimate=pl.CostEstimate(flops=cost, bytes_accessed=cost // 200, transcendentals=0),
        name=name,
    )


def pair_grads(n_freq, n_subj, slots_of, blocks, time_table, second):
    cap, bt, cells = blocks.shape[3:]
    n_ta, rows, rank = second.shape
    return kernel_call(
        functools.partial(pair_body, n_freq),
        jax.ShapeDtypeStruct(second.shape, SEND),
        [pltpu.SMEM, pltpu.HBM, pltpu.VMEM, pltpu.VMEM],
        [
            pltpu.VMEM((cap, bt, cells), BF16),
            pltpu.VMEM((6, rank, rank), F32),
            pltpu.VMEM((n_ta * n_freq, rank), F32),
            pltpu.VMEM((n_ta * n_subj, rank), F32),
            pltpu.SemaphoreType.DMA((cap,)),
        ],
        "pair_grads",
        2 * cap * bt * cells * rank,
        BIG,
    )(slots_of, blocks, time_table, second)


def time_grads(n_freq, slots_of, blocks, time_table, second):
    cap, bt, cells = blocks.shape[3:]
    rank = time_table.shape[1]
    return kernel_call(
        functools.partial(time_body, n_freq),
        jax.ShapeDtypeStruct((2, time_table.shape[0], HALF), F32),
        [pltpu.SMEM, pltpu.HBM, pltpu.VMEM, pltpu.VMEM],
        [
            pltpu.VMEM((cap, bt, cells), BF16),
            pltpu.VMEM(time_table.shape, F32),
            pltpu.SemaphoreType.DMA((cap,)),
        ],
        "time_grads",
        2 * cap * bt * cells * rank,
        BIG,
    )(slots_of, blocks, time_table, second)


def pack_grads(n_af, n_sa, got_ref, time_ref, out_ref, own_ref, summed, wide):
    af = lax.axis_index("af")
    slots = n_af * n_sa
    n_freq = ROWS * n_sa
    total = jnp.sum(got_ref[...].astype(F32), axis=0)
    for half in range(2):
        summed[half] = total[:, half * HALF : (half + 1) * HALF]
    for half in range(2):
        for row in range(ROWS):
            wide[pl.ds(2 * half + row, slots, stride=8), :] = time_ref[
                half, pl.ds(row, slots, stride=ROWS), :
            ]
            at = 4 + 2 * half + row
            for peer in range(n_af):
                there = n_freq + ROWS * peer + row
                subj = summed[half, there : there + 1, :]
                wide[pl.ds(peer * n_sa * 8 + at, n_sa, stride=8), :] = jnp.broadcast_to(
                    subj, (n_sa, HALF)
                )
            wide[pl.ds(af * (n_sa * 8) + at, n_sa, stride=8), :] = summed[
                half, pl.ds(row, n_sa, stride=ROWS), :
            ]
        own_ref[:, half * HALF : (half + 1) * HALF] = summed[
            half, pl.ds(n_freq + ROWS * af, ROWS), :
        ]
    out_ref[...] = wide[...].astype(SEND).reshape(slots, 8, HALF)


def update(
    n_af,
    n_sa,
    got_ref,
    own_ref,
    time_ref,
    freq_ref,
    subj_ref,
    time_vel_ref,
    freq_vel_ref,
    subj_vel_ref,
    new_time_ref,
    new_freq_ref,
    new_subj_ref,
    new_time_vel_ref,
    new_freq_vel_ref,
    new_subj_vel_ref,
):
    af = lax.axis_index("af")
    sa = lax.axis_index("sa")
    time = jnp.sum(got_ref[...].astype(F32), axis=0)
    freq = jnp.sum(got_ref[pl.ds(af * n_sa, n_sa)].astype(F32), axis=0)
    subj = jnp.zeros_like(freq)
    for peer in range(n_af):
        there = got_ref[peer * n_sa + sa].astype(F32)
        subj += jnp.where(peer == af, jnp.zeros_like(there), there)
    own = own_ref[...]
    for half in range(2):
        lanes = slice(half * HALF, (half + 1) * HALF)
        rows = slice(2 * half, 2 * half + 2)
        more = slice(4 + 2 * half, 6 + 2 * half)
        for grad, old, vel, new, new_vel in (
            (time[rows], time_ref, time_vel_ref, new_time_ref, new_time_vel_ref),
            (freq[more], freq_ref, freq_vel_ref, new_freq_ref, new_freq_vel_ref),
            (subj[more] + own[:, lanes], subj_ref, subj_vel_ref, new_subj_ref, new_subj_vel_ref),
        ):
            velocity = 0.9 * vel[0, :, lanes] + grad / 64.0
            new_vel[0, :, lanes] = velocity
            new[0, :, lanes] = old[0, :, lanes] - 0.5 * velocity


def per_device(sizes, *args):
    n_ta, n_af, n_sa = sizes
    blocks, coords, counts, time, freq, subj, time_vel, freq_vel, subj_vel = args
    slots = n_af * n_sa
    rank = time.shape[-1]
    pair_rows = ROWS * (n_sa + n_af)
    table = ROWS * slots
    coords = coords.transpose(0, 1, 2, 4, 3).reshape(3, -1)
    slots_of = jnp.concatenate([coords, jnp.broadcast_to(counts.reshape(1, 1), (1, coords.shape[1]))])

    packed = pl.pallas_call(
        functools.partial(pack_factors, n_sa),
        out_shape=jax.ShapeDtypeStruct((slots, 8, HALF), BF16),
        scratch_shapes=[pltpu.VMEM((8, HALF), F32)] * 2,
        compiler_params=pltpu.CompilerParams(vmem_limit_bytes=SMALL),
        name="pack_factors",
    )(jnp.concatenate([time, freq, subj], axis=0))
    first = lax.all_to_all(packed, ("af", "sa"), 0, 0, tiled=True)
    joined, time_table = pl.pallas_call(
        functools.partial(join_factors, n_af, n_sa),
        out_shape=[
            jax.ShapeDtypeStruct((n_ta, pair_rows, rank), BF16),
            jax.ShapeDtypeStruct((table, rank), BF16),
        ],
        scratch_shapes=[
            pltpu.VMEM((slots * 8, HALF), F32),
            pltpu.VMEM((2, pair_rows, HALF), F32),
            pltpu.VMEM((2, table, HALF), F32),
        ],
        compiler_params=pltpu.CompilerParams(vmem_limit_bytes=SMALL),
        name="join_factors",
    )(first, packed)
    second = lax.all_to_all(joined, "ta", 0, 0, tiled=True)
    pair = pair_grads(ROWS * n_sa, ROWS * n_af, slots_of, blocks, time_table, second)
    time_grad = time_grads(ROWS * n_sa, slots_of, blocks, time_table, second)
    third = lax.all_to_all(pair, "ta", 0, 0, tiled=True)
    packed_grads, own = pl.pallas_call(
        functools.partial(pack_grads, n_af, n_sa),
        out_shape=[
            jax.ShapeDtypeStruct((slots, 8, HALF), SEND),
            jax.ShapeDtypeStruct((ROWS, rank), F32),
        ],
        scratch_shapes=[
            pltpu.VMEM((2, pair_rows, HALF), F32),
            pltpu.VMEM((slots * 8, HALF), F32),
        ],
        compiler_params=pltpu.CompilerParams(vmem_limit_bytes=SMALL),
        name="pack_grads",
    )(third, time_grad)
    fourth = lax.all_to_all(packed_grads, ("af", "sa"), 0, 0, tiled=True)
    return pl.pallas_call(
        functools.partial(update, n_af, n_sa),
        out_shape=[jax.ShapeDtypeStruct(time.shape, F32)] * 6,
        compiler_params=pltpu.CompilerParams(vmem_limit_bytes=SMALL),
        name="update",
    )(fourth, own, time, freq, subj, time_vel, freq_vel, subj_vel)


def solution(mesh):
    sizes = tuple(mesh.shape[name] for name in ("ta", "af", "sa"))
    factors = (P("ta", ("af", "sa"), None), P("af", ("ta", "sa"), None), P("sa", ("ta", "af"), None))
    return jax.shard_map(
        lambda *args: tuple(per_device(sizes, *args)),
        mesh=mesh,
        in_specs=(
            P("ta", "af", "sa", None, None, None),
            P("ta", "af", "sa", None, None),
            P("ta", "af", "sa"),
            *factors,
            *factors,
        ),
        out_specs=(*factors, *factors),
        check_vma=False,
    )
```

```python
import functools

import jax
import jax.numpy as jnp
from jax import lax
from jax.experimental import pallas as pl
from jax.experimental.pallas import tpu as pltpu
from jax.sharding import PartitionSpec as P

BF16 = jnp.bfloat16
F32 = jnp.float32
ROWS = 2
HALF = 128
BIG = 24 << 20
FETCH = 53 * 1000 * 1000
SMALL = 4 << 20
SEND = BF16


def put_rows(tile, at, rows):
    tile[at : at + 2, :] = rows[:, :HALF]
    tile[at + 2 : at + 4, :] = rows[:, HALF:]


def pack_factors(n_sa, own_ref, out_ref, with_freq, with_subj):
    mine = lax.axis_index("af")
    put_rows(with_freq, 0, own_ref[0])
    put_rows(with_subj, 0, own_ref[0])
    put_rows(with_freq, 4, own_ref[1])
    put_rows(with_subj, 4, own_ref[2])
    freq_tile = with_freq[...].astype(BF16)
    subj_tile = with_subj[...].astype(BF16)
    out_ref[...] = jnp.broadcast_to(subj_tile[None], out_ref.shape)
    out_ref[pl.ds(mine * n_sa, n_sa)] = jnp.broadcast_to(freq_tile[None], (n_sa, 8, HALF))


def join_factors(n_af, n_sa, got_ref, packed_ref, out_ref, time_ref, wide, joined, time_table):
    af = lax.axis_index("af")
    sa = lax.axis_index("sa")
    slots = n_af * n_sa
    wide[...] = got_ref[...].astype(F32).reshape(slots * 8, HALF)
    own = packed_ref[jnp.where(af == 0, n_sa, 0)].astype(F32)
    is_own = lax.broadcasted_iota(jnp.int32, (n_af, HALF), 0) == af
    for half in range(2):
        for row in range(ROWS):
            at = 4 + 2 * half + row
            freq = wide[pl.ds(af * (n_sa * 8) + at, n_sa, stride=8), :]
            joined[half, pl.ds(row, n_sa, stride=ROWS), :] = freq
            subj = wide[pl.ds(sa * 8 + at, n_af, stride=n_sa * 8), :]
            subj = jnp.where(is_own, own[at : at + 1], subj)
            joined[half, pl.ds(ROWS * n_sa + row, n_af, stride=ROWS), :] = subj
    rows = jnp.concatenate([joined[0], joined[1]], axis=1).astype(BF16)
    for peer in range(out_ref.shape[0]):
        out_ref[peer] = rows
    for half in range(2):
        for row in range(ROWS):
            time_table[half, pl.ds(row, slots, stride=ROWS), :] = wide[
                pl.ds(2 * half + row, slots, stride=8), :
            ]
    time_ref[...] = jnp.concatenate([time_table[0], time_table[1]], axis=1).astype(BF16)


def dot(a, b, contract=((1,), (0,))):
    return lax.dot_general(a, b, (contract, ((), ())), preferred_element_type=F32)


def gram(table):
    return dot(table, table, ((0,), (0,)))


def model_part(rows, grams):
    high = grams.astype(BF16)
    low = (grams - high.astype(F32)).astype(BF16)
    return dot(rows, high) + dot(rows, low)


def take(ref, which, extent):
    return ref[pl.ds(pl.multiple_of(which * extent, extent), extent), :]


def pair_blocks(ref, freq_at, subj_at, n_freq):
    half_ta = ref.shape[0] // 2
    rank = ref.shape[2]
    freq = ref[pl.ds(freq_at * half_ta, half_ta), :n_freq, :]
    subj = ref[pl.ds(subj_at * half_ta, half_ta), n_freq:, :]
    return freq.reshape(-1, rank), subj.reshape(-1, rank)


def fetch_body(blocks_ref, time_ref, data_ref, grams_ref, sems):
    cap, bt, cells = data_ref.shape
    parts = sems.shape[1]
    rows = bt // parts
    copies = [
        pltpu.make_async_copy(
            blocks_ref.at[0, 0, 0, slot, pl.ds(part * rows, rows)],
            data_ref.at[slot, pl.ds(part * rows, rows)],
            sems.at[slot, part],
        )
        for slot in range(cap)
        for part in range(parts)
    ]
    for copy in copies:
        copy.start()
    for which in range(2):
        grams_ref[which] = gram(take(time_ref, which, time_ref.shape[0] // 2))
    for copy in copies:
        copy.wait()


def pair_body(
    n_freq,
    where_ref,
    data_ref,
    time_ref,
    time_grams_ref,
    second_ref,
    pair_ref,
    grams,
    freq,
    subj,
):
    n_ta = second_ref.shape[0]
    bf = freq.shape[0] // 2
    bs = subj.shape[0] // 2
    bt = time_ref.shape[0] // 2
    n_subj = second_ref.shape[1] - n_freq
    freq[...] = jnp.zeros_like(freq)
    subj[...] = jnp.zeros_like(subj)
    for which in range(2):
        b, c = pair_blocks(second_ref, which, which, n_freq)
        grams[which] = gram(b)
        grams[2 + which] = gram(c)
    step = min(8, bf)
    for slot in range(data_ref.shape[0]):
        live = slot < where_ref[3, slot]
        time_at = where_ref[0, slot]
        freq_at = where_ref[1, slot]
        subj_at = where_ref[2, slot]
        a = take(time_ref, time_at, bt)
        b, c = pair_blocks(second_ref, freq_at, subj_at, n_freq)
        time_gram = time_grams_ref[time_at]
        freq_model = model_part(b, time_gram * grams[2 + subj_at])
        subj_model = model_part(c, time_gram * grams[freq_at])
        wide_b, wide_c = b.astype(F32), c.astype(F32)
        freq_data = []
        subj_data = jnp.zeros(wide_c.shape, F32)
        for j in range(0, bf, step):
            cells = data_ref[slot, :, j * bs : (j + step) * bs]
            cube = dot(cells, a, ((0,), (0,))).reshape(step, bs, -1)
            freq_data.append(jnp.sum(cube * wide_c[None], axis=1))
            for k in range(step):
                subj_data += cube[k] * wide_b[j + k : j + k + 1]
        freq_data = jnp.concatenate(freq_data, axis=0)
        freq_grad = jnp.where(live, freq_model - freq_data, 0.0)
        subj_grad = jnp.where(live, subj_model - subj_data, 0.0)
        freq[pl.ds(pl.multiple_of(freq_at * bf, bf), bf), :] += freq_grad
        subj[pl.ds(pl.multiple_of(subj_at * bs, bs), bs), :] += subj_grad

    for t in range(n_ta):
        pair_ref[t, :n_freq, :] = freq[t * n_freq : (t + 1) * n_freq, :].astype(SEND)
        pair_ref[t, n_freq:, :] = subj[t * n_subj : (t + 1) * n_subj, :].astype(SEND)


def time_body(n_freq, where_ref, data_ref, time_ref, second_ref, out_ref, grad):
    bt = data_ref.shape[1]
    grad[...] = jnp.zeros_like(grad)
    for slot in range(data_ref.shape[0]):
        live = slot < where_ref[3, slot]
        time_at = where_ref[0, slot]
        a = take(time_ref, time_at, bt)
        b, c = pair_blocks(second_ref, where_ref[1, slot], where_ref[2, slot], n_freq)
        bf, bs = b.shape[0], c.shape[0]
        step = min(8, bf)
        total = model_part(a, gram(b) * gram(c))
        for j in range(0, bf, step):
            khatri = (b[j : j + step][:, None, :] * c[None]).reshape(step * bs, -1)
            total -= dot(data_ref[slot, :, j * bs : (j + step) * bs], khatri)
        grad[pl.ds(pl.multiple_of(time_at * bt, bt), bt), :] += jnp.where(live, total, 0.0)

    for half in range(2):
        out_ref[half] = grad[:, half * HALF : (half + 1) * HALF]


def kernel_call(body, out_shape, in_spaces, scratch, name, cost, limit):
    return pl.pallas_call(
        body,
        out_shape=out_shape,
        in_specs=[pl.BlockSpec(memory_space=space) for space in in_spaces],
        out_specs=jax.tree.map(lambda _: pl.BlockSpec(memory_space=pltpu.VMEM), out_shape),
        scratch_shapes=scratch,
        compiler_params=pltpu.CompilerParams(vmem_limit_bytes=limit),
        cost_estimate=pl.CostEstimate(flops=cost, bytes_accessed=cost // 200, transcendentals=0),
        name=name,
    )


def fetch(blocks, time_table):
    cap, bt, cells = blocks.shape[3:]
    rank = time_table.shape[1]
    return kernel_call(
        fetch_body,
        [
            jax.ShapeDtypeStruct((cap, bt, cells), BF16),
            jax.ShapeDtypeStruct((2, rank, rank), F32),
        ],
        [pltpu.HBM, pltpu.VMEM],
        [pltpu.SemaphoreType.DMA((cap, 4))],
        "fetch",
        cap * bt * cells * 4,
        FETCH,
    )(blocks, time_table)


def pair_grads(n_freq, n_subj, slots_of, data, time_table, time_grams, second):
    n_ta, rows, rank = second.shape
    return kernel_call(
        functools.partial(pair_body, n_freq),
        jax.ShapeDtypeStruct(second.shape, SEND),
        [pltpu.SMEM] + [pltpu.VMEM] * 4,
        [
            pltpu.VMEM((4, rank, rank), F32),
            pltpu.VMEM((n_ta * n_freq, rank), F32),
            pltpu.VMEM((n_ta * n_subj, rank), F32),
        ],
        "pair_grads",
        2 * data.size * rank,
        BIG,
    )(slots_of, data, time_table, time_grams, second)


def time_grads(n_freq, slots_of, data, time_table, second):
    return kernel_call(
        functools.partial(time_body, n_freq),
        jax.ShapeDtypeStruct((2, time_table.shape[0], HALF), F32),
        [pltpu.SMEM] + [pltpu.VMEM] * 3,
        [pltpu.VMEM(time_table.shape, F32)],
        "time_grads",
        2 * data.size * time_table.shape[1],
        BIG,
    )(slots_of, data, time_table, second)


def pack_grads(n_af, n_sa, got_ref, time_ref, out_ref, own_ref, summed, wide):
    af = lax.axis_index("af")
    slots = n_af * n_sa
    n_freq = ROWS * n_sa
    total = jnp.sum(got_ref[...].astype(F32), axis=0)
    for half in range(2):
        summed[half] = total[:, half * HALF : (half + 1) * HALF]
    for half in range(2):
        for row in range(ROWS):
            wide[pl.ds(2 * half + row, slots, stride=8), :] = time_ref[
                half, pl.ds(row, slots, stride=ROWS), :
            ]
            at = 4 + 2 * half + row
            for peer in range(n_af):
                there = n_freq + ROWS * peer + row
                subj = summed[half, there : there + 1, :]
                wide[pl.ds(peer * n_sa * 8 + at, n_sa, stride=8), :] = jnp.broadcast_to(
                    subj, (n_sa, HALF)
                )
            wide[pl.ds(af * (n_sa * 8) + at, n_sa, stride=8), :] = summed[
                half, pl.ds(row, n_sa, stride=ROWS), :
            ]
        own_ref[:, half * HALF : (half + 1) * HALF] = summed[
            half, pl.ds(n_freq + ROWS * af, ROWS), :
        ]
    out_ref[...] = wide[...].astype(SEND).reshape(slots, 8, HALF)


def update(
    n_af,
    n_sa,
    got_ref,
    own_ref,
    time_ref,
    freq_ref,
    subj_ref,
    time_vel_ref,
    freq_vel_ref,
    subj_vel_ref,
    new_time_ref,
    new_freq_ref,
    new_subj_ref,
    new_time_vel_ref,
    new_freq_vel_ref,
    new_subj_vel_ref,
):
    af = lax.axis_index("af")
    sa = lax.axis_index("sa")
    time = jnp.sum(got_ref[...].astype(F32), axis=0)
    freq = jnp.sum(got_ref[pl.ds(af * n_sa, n_sa)].astype(F32), axis=0)
    subj = jnp.zeros_like(freq)
    for peer in range(n_af):
        there = got_ref[peer * n_sa + sa].astype(F32)
        subj += jnp.where(peer == af, jnp.zeros_like(there), there)
    own = own_ref[...]
    for half in range(2):
        lanes = slice(half * HALF, (half + 1) * HALF)
        rows = slice(2 * half, 2 * half + 2)
        more = slice(4 + 2 * half, 6 + 2 * half)
        for grad, old, vel, new, new_vel in (
            (time[rows], time_ref, time_vel_ref, new_time_ref, new_time_vel_ref),
            (freq[more], freq_ref, freq_vel_ref, new_freq_ref, new_freq_vel_ref),
            (subj[more] + own[:, lanes], subj_ref, subj_vel_ref, new_subj_ref, new_subj_vel_ref),
        ):
            velocity = 0.9 * vel[0, :, lanes] + grad / 64.0
            new_vel[0, :, lanes] = velocity
            new[0, :, lanes] = old[0, :, lanes] - 0.5 * velocity


def per_device(sizes, *args):
    n_ta, n_af, n_sa = sizes
    blocks, coords, counts, time, freq, subj, time_vel, freq_vel, subj_vel = args
    slots = n_af * n_sa
    rank = time.shape[-1]
    pair_rows = ROWS * (n_sa + n_af)
    table = ROWS * slots
    coords = coords.transpose(0, 1, 2, 4, 3).reshape(3, -1)
    slots_of = jnp.concatenate([coords, jnp.broadcast_to(counts.reshape(1, 1), (1, coords.shape[1]))])

    packed = pl.pallas_call(
        functools.partial(pack_factors, n_sa),
        out_shape=jax.ShapeDtypeStruct((slots, 8, HALF), BF16),
        scratch_shapes=[pltpu.VMEM((8, HALF), F32)] * 2,
        compiler_params=pltpu.CompilerParams(vmem_limit_bytes=SMALL),
        name="pack_factors",
    )(jnp.concatenate([time, freq, subj], axis=0))
    first = lax.all_to_all(packed, ("af", "sa"), 0, 0, tiled=True)
    joined, time_table = pl.pallas_call(
        functools.partial(join_factors, n_af, n_sa),
        out_shape=[
            jax.ShapeDtypeStruct((n_ta, pair_rows, rank), BF16),
            jax.ShapeDtypeStruct((table, rank), BF16),
        ],
        scratch_shapes=[
            pltpu.VMEM((slots * 8, HALF), F32),
            pltpu.VMEM((2, pair_rows, HALF), F32),
            pltpu.VMEM((2, table, HALF), F32),
        ],
        compiler_params=pltpu.CompilerParams(vmem_limit_bytes=SMALL),
        name="join_factors",
    )(first, packed)
    second = lax.all_to_all(joined, "ta", 0, 0, tiled=True)
    data, time_grams = fetch(blocks, time_table)
    n_freq, n_subj = ROWS * n_sa, ROWS * n_af
    pair = pair_grads(n_freq, n_subj, slots_of, data, time_table, time_grams, second)
    time_grad = time_grads(n_freq, slots_of, data, time_table, second)
    third = lax.all_to_all(pair, "ta", 0, 0, tiled=True)
    packed_grads, own = pl.pallas_call(
        functools.partial(pack_grads, n_af, n_sa),
        out_shape=[
            jax.ShapeDtypeStruct((slots, 8, HALF), SEND),
            jax.ShapeDtypeStruct((ROWS, rank), F32),
        ],
        scratch_shapes=[
            pltpu.VMEM((2, pair_rows, HALF), F32),
            pltpu.VMEM((slots * 8, HALF), F32),
        ],
        compiler_params=pltpu.CompilerParams(vmem_limit_bytes=SMALL),
        name="pack_grads",
    )(third, time_grad)
    fourth = lax.all_to_all(packed_grads, ("af", "sa"), 0, 0, tiled=True)
    return pl.pallas_call(
        functools.partial(update, n_af, n_sa),
        out_shape=[jax.ShapeDtypeStruct(time.shape, F32)] * 6,
        compiler_params=pltpu.CompilerParams(vmem_limit_bytes=SMALL),
        name="update",
    )(fourth, own, time, freq, subj, time_vel, freq_vel, subj_vel)


def solution(mesh):
    sizes = tuple(mesh.shape[name] for name in ("ta", "af", "sa"))
    factors = (P("ta", ("af", "sa"), None), P("af", ("ta", "sa"), None), P("sa", ("ta", "af"), None))
    return jax.shard_map(
        lambda *args: tuple(per_device(sizes, *args)),
        mesh=mesh,
        in_specs=(
            P("ta", "af", "sa", None, None, None),
            P("ta", "af", "sa", None, None),
            P("ta", "af", "sa"),
            *factors,
            *factors,
        ),
        out_specs=(*factors, *factors),
        check_vma=False,
    )
```

```python
import functools

import jax
import jax.numpy as jnp
from jax import lax
from jax.experimental import pallas as pl
from jax.experimental.pallas import tpu as pltpu
from jax.sharding import PartitionSpec as P

BF16 = jnp.bfloat16
F32 = jnp.float32
ROWS = 2
HALF = 128
BIG = 24 << 20
FETCH = 53 * 1000 * 1000
SMALL = 4 << 20
SEND = BF16


def put_rows(tile, at, rows):
    tile[at : at + 2, :] = rows[:, :HALF]
    tile[at + 2 : at + 4, :] = rows[:, HALF:]


def pack_factors(n_sa, own_ref, out_ref, with_freq, with_subj):
    mine = lax.axis_index("af")
    put_rows(with_freq, 0, own_ref[0])
    put_rows(with_subj, 0, own_ref[0])
    put_rows(with_freq, 4, own_ref[1])
    put_rows(with_subj, 4, own_ref[2])
    freq_tile = with_freq[...].astype(BF16)
    subj_tile = with_subj[...].astype(BF16)
    out_ref[...] = jnp.broadcast_to(subj_tile[None], out_ref.shape)
    out_ref[pl.ds(mine * n_sa, n_sa)] = jnp.broadcast_to(freq_tile[None], (n_sa, 8, HALF))


def join_factors(n_af, n_sa, got_ref, packed_ref, out_ref, wide, joined):
    af = lax.axis_index("af")
    sa = lax.axis_index("sa")
    slots = n_af * n_sa
    wide[...] = got_ref[...].astype(F32).reshape(slots * 8, HALF)
    own = packed_ref[jnp.where(af == 0, n_sa, 0)].astype(F32)
    is_own = lax.broadcasted_iota(jnp.int32, (n_af, HALF), 0) == af
    for half in range(2):
        for row in range(ROWS):
            at = 4 + 2 * half + row
            freq = wide[pl.ds(af * (n_sa * 8) + at, n_sa, stride=8), :]
            joined[half, pl.ds(row, n_sa, stride=ROWS), :] = freq
            subj = wide[pl.ds(sa * 8 + at, n_af, stride=n_sa * 8), :]
            subj = jnp.where(is_own, own[at : at + 1], subj)
            joined[half, pl.ds(ROWS * n_sa + row, n_af, stride=ROWS), :] = subj
    rows = jnp.concatenate([joined[0], joined[1]], axis=1).astype(BF16)
    for peer in range(out_ref.shape[0]):
        out_ref[peer] = rows


def dot(a, b, contract=((1,), (0,))):
    return lax.dot_general(a, b, (contract, ((), ())), preferred_element_type=F32)


def gram(table):
    return dot(table, table, ((0,), (0,)))


def model_part(rows, grams):
    high = grams.astype(BF16)
    low = (grams - high.astype(F32)).astype(BF16)
    return dot(rows, high) + dot(rows, low)


def take(ref, which, extent):
    return ref[pl.ds(pl.multiple_of(which * extent, extent), extent), :]


def pair_blocks(ref, freq_at, subj_at, n_freq):
    half_ta = ref.shape[0] // 2
    rank = ref.shape[2]
    freq = ref[pl.ds(freq_at * half_ta, half_ta), :n_freq, :]
    subj = ref[pl.ds(subj_at * half_ta, half_ta), n_freq:, :]
    return freq.reshape(-1, rank), subj.reshape(-1, rank)


def fetch_body(blocks_ref, got_ref, data_ref, grams_ref, time_ref, sems, wide, time_table):
    cap, bt, cells = data_ref.shape
    parts = sems.shape[1]
    rows = bt // parts
    copies = [
        pltpu.make_async_copy(
            blocks_ref.at[0, 0, 0, slot, pl.ds(part * rows, rows)],
            data_ref.at[slot, pl.ds(part * rows, rows)],
            sems.at[slot, part],
        )
        for slot in range(cap)
        for part in range(parts)
    ]
    for copy in copies:
        copy.start()
    slots = got_ref.shape[0]
    wide[...] = got_ref[...].astype(F32).reshape(slots * 8, HALF)
    for half in range(2):
        for row in range(ROWS):
            time_table[half, pl.ds(row, slots, stride=ROWS), :] = wide[
                pl.ds(2 * half + row, slots, stride=8), :
            ]
    time_ref[...] = jnp.concatenate([time_table[0], time_table[1]], axis=1).astype(BF16)
    for which in range(2):
        grams_ref[which] = gram(take(time_ref, which, time_ref.shape[0] // 2))
    for copy in copies:
        copy.wait()


def pair_body(
    n_freq,
    where_ref,
    data_ref,
    time_ref,
    time_grams_ref,
    second_ref,
    pair_ref,
    grams,
    freq,
    subj,
):
    n_ta = second_ref.shape[0]
    bf = freq.shape[0] // 2
    bs = subj.shape[0] // 2
    bt = time_ref.shape[0] // 2
    n_subj = second_ref.shape[1] - n_freq
    freq[...] = jnp.zeros_like(freq)
    subj[...] = jnp.zeros_like(subj)
    for which in range(2):
        b, c = pair_blocks(second_ref, which, which, n_freq)
        grams[which] = gram(b)
        grams[2 + which] = gram(c)
    step = min(8, bf)
    cap = data_ref.shape[0]
    tables = []
    for slot in range(cap):
        a = take(time_ref, where_ref[0, slot], bt)
        tables.append((a, *pair_blocks(second_ref, where_ref[1, slot], where_ref[2, slot], n_freq)))

    def product(slot, j):
        cells = data_ref[slot, :, j * bs : (j + step) * bs]
        return dot(cells, tables[slot][0], ((0,), (0,))).reshape(step, bs, -1)

    chunks = [(slot, j) for slot in range(cap) for j in range(0, bf, step)]
    ahead = product(*chunks[0])
    for at, (slot, j) in enumerate(chunks):
        cube = ahead
        if at + 1 < len(chunks):
            ahead = product(*chunks[at + 1])
        a, b, c = tables[slot]
        if j == 0:
            wide_b, wide_c = b.astype(F32), c.astype(F32)
            freq_data = []
            subj_data = jnp.zeros(wide_c.shape, F32)
        freq_data.append(jnp.sum(cube * wide_c[None], axis=1))
        for k in range(step):
            subj_data += cube[k] * wide_b[j + k : j + k + 1]
        if j + step == bf:
            live = slot < where_ref[3, slot]
            freq_at, subj_at = where_ref[1, slot], where_ref[2, slot]
            time_gram = time_grams_ref[where_ref[0, slot]]
            freq_grad = model_part(b, time_gram * grams[2 + subj_at])
            subj_grad = model_part(c, time_gram * grams[freq_at])
            freq_grad = jnp.where(live, freq_grad - jnp.concatenate(freq_data, axis=0), 0.0)
            subj_grad = jnp.where(live, subj_grad - subj_data, 0.0)
            freq[pl.ds(pl.multiple_of(freq_at * bf, bf), bf), :] += freq_grad
            subj[pl.ds(pl.multiple_of(subj_at * bs, bs), bs), :] += subj_grad

    for t in range(n_ta):
        pair_ref[t, :n_freq, :] = freq[t * n_freq : (t + 1) * n_freq, :].astype(SEND)
        pair_ref[t, n_freq:, :] = subj[t * n_subj : (t + 1) * n_subj, :].astype(SEND)


def time_body(n_freq, where_ref, data_ref, time_ref, second_ref, out_ref, grad):
    bt = data_ref.shape[1]
    grad[...] = jnp.zeros_like(grad)
    for slot in range(data_ref.shape[0]):
        live = slot < where_ref[3, slot]
        time_at = where_ref[0, slot]
        a = take(time_ref, time_at, bt)
        b, c = pair_blocks(second_ref, where_ref[1, slot], where_ref[2, slot], n_freq)
        bf, bs = b.shape[0], c.shape[0]
        step = min(8, bf)
        total = model_part(a, gram(b) * gram(c))
        for j in range(0, bf, step):
            khatri = (b[j : j + step][:, None, :] * c[None]).reshape(step * bs, -1)
            total -= dot(data_ref[slot, :, j * bs : (j + step) * bs], khatri)
        grad[pl.ds(pl.multiple_of(time_at * bt, bt), bt), :] += jnp.where(live, total, 0.0)

    for half in range(2):
        out_ref[half] = grad[:, half * HALF : (half + 1) * HALF]


def kernel_call(body, out_shape, in_spaces, scratch, name, cost, limit):
    return pl.pallas_call(
        body,
        out_shape=out_shape,
        in_specs=[pl.BlockSpec(memory_space=space) for space in in_spaces],
        out_specs=jax.tree.map(lambda _: pl.BlockSpec(memory_space=pltpu.VMEM), out_shape),
        scratch_shapes=scratch,
        compiler_params=pltpu.CompilerParams(vmem_limit_bytes=limit),
        cost_estimate=pl.CostEstimate(flops=cost, bytes_accessed=cost // 200, transcendentals=0),
        name=name,
    )


def fetch(blocks, first):
    cap, bt, cells = blocks.shape[3:]
    slots = first.shape[0]
    table, rank = ROWS * slots, 2 * HALF
    return kernel_call(
        fetch_body,
        [
            jax.ShapeDtypeStruct((cap, bt, cells), BF16),
            jax.ShapeDtypeStruct((2, rank, rank), F32),
            jax.ShapeDtypeStruct((table, rank), BF16),
        ],
        [pltpu.HBM, pltpu.VMEM],
        [
            pltpu.SemaphoreType.DMA((cap, 4)),
            pltpu.VMEM((slots * 8, HALF), F32),
            pltpu.VMEM((2, table, HALF), F32),
        ],
        "fetch",
        cap * bt * cells * 4,
        FETCH,
    )(blocks, first)


def pair_grads(n_freq, n_subj, slots_of, data, time_table, time_grams, second):
    n_ta, rows, rank = second.shape
    return kernel_call(
        functools.partial(pair_body, n_freq),
        jax.ShapeDtypeStruct(second.shape, SEND),
        [pltpu.SMEM] + [pltpu.VMEM] * 4,
        [
            pltpu.VMEM((4, rank, rank), F32),
            pltpu.VMEM((n_ta * n_freq, rank), F32),
            pltpu.VMEM((n_ta * n_subj, rank), F32),
        ],
        "pair_grads",
        2 * data.size * rank,
        BIG,
    )(slots_of, data, time_table, time_grams, second)


def time_grads(n_freq, slots_of, data, time_table, second):
    return kernel_call(
        functools.partial(time_body, n_freq),
        jax.ShapeDtypeStruct((2, time_table.shape[0], HALF), F32),
        [pltpu.SMEM] + [pltpu.VMEM] * 3,
        [pltpu.VMEM(time_table.shape, F32)],
        "time_grads",
        2 * data.size * time_table.shape[1],
        BIG,
    )(slots_of, data, time_table, second)


def pack_grads(n_af, n_sa, got_ref, time_ref, out_ref, own_ref, summed, wide):
    af = lax.axis_index("af")
    slots = n_af * n_sa
    n_freq = ROWS * n_sa
    total = jnp.sum(got_ref[...].astype(F32), axis=0)
    for half in range(2):
        summed[half] = total[:, half * HALF : (half + 1) * HALF]
    for half in range(2):
        for row in range(ROWS):
            wide[pl.ds(2 * half + row, slots, stride=8), :] = time_ref[
                half, pl.ds(row, slots, stride=ROWS), :
            ]
            at = 4 + 2 * half + row
            for peer in range(n_af):
                there = n_freq + ROWS * peer + row
                subj = summed[half, there : there + 1, :]
                wide[pl.ds(peer * n_sa * 8 + at, n_sa, stride=8), :] = jnp.broadcast_to(
                    subj, (n_sa, HALF)
                )
            wide[pl.ds(af * (n_sa * 8) + at, n_sa, stride=8), :] = summed[
                half, pl.ds(row, n_sa, stride=ROWS), :
            ]
        own_ref[:, half * HALF : (half + 1) * HALF] = summed[
            half, pl.ds(n_freq + ROWS * af, ROWS), :
        ]
    out_ref[...] = wide[...].astype(SEND).reshape(slots, 8, HALF)


def update(
    n_af,
    n_sa,
    got_ref,
    own_ref,
    time_ref,
    freq_ref,
    subj_ref,
    time_vel_ref,
    freq_vel_ref,
    subj_vel_ref,
    new_time_ref,
    new_freq_ref,
    new_subj_ref,
    new_time_vel_ref,
    new_freq_vel_ref,
    new_subj_vel_ref,
):
    af = lax.axis_index("af")
    sa = lax.axis_index("sa")
    time = jnp.sum(got_ref[...].astype(F32), axis=0)
    freq = jnp.sum(got_ref[pl.ds(af * n_sa, n_sa)].astype(F32), axis=0)
    subj = jnp.zeros_like(freq)
    for peer in range(n_af):
        there = got_ref[peer * n_sa + sa].astype(F32)
        subj += jnp.where(peer == af, jnp.zeros_like(there), there)
    own = own_ref[...]
    for half in range(2):
        lanes = slice(half * HALF, (half + 1) * HALF)
        rows = slice(2 * half, 2 * half + 2)
        more = slice(4 + 2 * half, 6 + 2 * half)
        for grad, old, vel, new, new_vel in (
            (time[rows], time_ref, time_vel_ref, new_time_ref, new_time_vel_ref),
            (freq[more], freq_ref, freq_vel_ref, new_freq_ref, new_freq_vel_ref),
            (subj[more] + own[:, lanes], subj_ref, subj_vel_ref, new_subj_ref, new_subj_vel_ref),
        ):
            velocity = 0.9 * vel[0, :, lanes] + grad / 64.0
            new_vel[0, :, lanes] = velocity
            new[0, :, lanes] = old[0, :, lanes] - 0.5 * velocity


def per_device(sizes, *args):
    n_ta, n_af, n_sa = sizes
    blocks, coords, counts, time, freq, subj, time_vel, freq_vel, subj_vel = args
    slots = n_af * n_sa
    rank = time.shape[-1]
    pair_rows = ROWS * (n_sa + n_af)
    coords = coords.transpose(0, 1, 2, 4, 3).reshape(3, -1)
    slots_of = jnp.concatenate([coords, jnp.broadcast_to(counts.reshape(1, 1), (1, coords.shape[1]))])

    packed = pl.pallas_call(
        functools.partial(pack_factors, n_sa),
        out_shape=jax.ShapeDtypeStruct((slots, 8, HALF), BF16),
        scratch_shapes=[pltpu.VMEM((8, HALF), F32)] * 2,
        compiler_params=pltpu.CompilerParams(vmem_limit_bytes=SMALL),
        name="pack_factors",
    )(jnp.concatenate([time, freq, subj], axis=0))
    first = lax.all_to_all(packed, ("af", "sa"), 0, 0, tiled=True)
    joined = pl.pallas_call(
        functools.partial(join_factors, n_af, n_sa),
        out_shape=jax.ShapeDtypeStruct((n_ta, pair_rows, rank), BF16),
        scratch_shapes=[
            pltpu.VMEM((slots * 8, HALF), F32),
            pltpu.VMEM((2, pair_rows, HALF), F32),
        ],
        compiler_params=pltpu.CompilerParams(vmem_limit_bytes=SMALL),
        name="join_factors",
    )(first, packed)
    second = lax.all_to_all(joined, "ta", 0, 0, tiled=True)
    data, time_grams, time_table = fetch(blocks, first)
    n_freq, n_subj = ROWS * n_sa, ROWS * n_af
    pair = pair_grads(n_freq, n_subj, slots_of, data, time_table, time_grams, second)
    time_grad = time_grads(n_freq, slots_of, data, time_table, second)
    third = lax.all_to_all(pair, "ta", 0, 0, tiled=True)
    packed_grads, own = pl.pallas_call(
        functools.partial(pack_grads, n_af, n_sa),
        out_shape=[
            jax.ShapeDtypeStruct((slots, 8, HALF), SEND),
            jax.ShapeDtypeStruct((ROWS, rank), F32),
        ],
        scratch_shapes=[
            pltpu.VMEM((2, pair_rows, HALF), F32),
            pltpu.VMEM((slots * 8, HALF), F32),
        ],
        compiler_params=pltpu.CompilerParams(vmem_limit_bytes=SMALL),
        name="pack_grads",
    )(third, time_grad)
    fourth = lax.all_to_all(packed_grads, ("af", "sa"), 0, 0, tiled=True)
    return pl.pallas_call(
        functools.partial(update, n_af, n_sa),
        out_shape=[jax.ShapeDtypeStruct(time.shape, F32)] * 6,
        compiler_params=pltpu.CompilerParams(vmem_limit_bytes=SMALL),
        name="update",
    )(fourth, own, time, freq, subj, time_vel, freq_vel, subj_vel)


def solution(mesh):
    sizes = tuple(mesh.shape[name] for name in ("ta", "af", "sa"))
    factors = (P("ta", ("af", "sa"), None), P("af", ("ta", "sa"), None), P("sa", ("ta", "af"), None))
    return jax.shard_map(
        lambda *args: tuple(per_device(sizes, *args)),
        mesh=mesh,
        in_specs=(
            P("ta", "af", "sa", None, None, None),
            P("ta", "af", "sa", None, None),
            P("ta", "af", "sa"),
            *factors,
            *factors,
        ),
        out_specs=(*factors, *factors),
        check_vma=False,
    )
```

```python
import functools

import jax
import jax.numpy as jnp
from jax import lax
from jax.experimental import pallas as pl
from jax.experimental.pallas import tpu as pltpu
from jax.sharding import PartitionSpec as P

BF16 = jnp.bfloat16
F32 = jnp.float32
ROWS = 2
HALF = 128
BIG = 24 << 20
FETCH = 53 * 1000 * 1000
SMALL = 4 << 20
SEND = BF16


def put_rows(tile, at, rows):
    tile[at : at + 2, :] = rows[:, :HALF]
    tile[at + 2 : at + 4, :] = rows[:, HALF:]


def pack_factors(n_sa, own_ref, out_ref, with_freq, with_subj):
    mine = lax.axis_index("af")
    put_rows(with_freq, 0, own_ref[0])
    put_rows(with_subj, 0, own_ref[0])
    put_rows(with_freq, 4, own_ref[1])
    put_rows(with_subj, 4, own_ref[2])
    freq_tile = with_freq[...].astype(BF16)
    subj_tile = with_subj[...].astype(BF16)
    out_ref[...] = jnp.broadcast_to(subj_tile[None], out_ref.shape)
    out_ref[pl.ds(mine * n_sa, n_sa)] = jnp.broadcast_to(freq_tile[None], (n_sa, 8, HALF))


def join_factors(n_af, n_sa, got_ref, packed_ref, out_ref, wide, joined, rows, sems):
    af = lax.axis_index("af")
    sa = lax.axis_index("sa")
    slots = n_af * n_sa
    wide[...] = got_ref[...].astype(F32).reshape(slots * 8, HALF)
    own = packed_ref[jnp.where(af == 0, n_sa, 0)].astype(F32)
    is_own = lax.broadcasted_iota(jnp.int32, (n_af, HALF), 0) == af
    for half in range(2):
        for row in range(ROWS):
            at = 4 + 2 * half + row
            freq = wide[pl.ds(af * (n_sa * 8) + at, n_sa, stride=8), :]
            joined[half, pl.ds(row, n_sa, stride=ROWS), :] = freq
            subj = wide[pl.ds(sa * 8 + at, n_af, stride=n_sa * 8), :]
            subj = jnp.where(is_own, own[at : at + 1], subj)
            joined[half, pl.ds(ROWS * n_sa + row, n_af, stride=ROWS), :] = subj
    rows[...] = jnp.concatenate([joined[0], joined[1]], axis=1).astype(BF16)
    copies = [
        pltpu.make_async_copy(rows, out_ref.at[peer], sems.at[peer])
        for peer in range(out_ref.shape[0])
    ]
    for copy in copies:
        copy.start()
    for copy in copies:
        copy.wait()


def dot(a, b, contract=((1,), (0,))):
    return lax.dot_general(a, b, (contract, ((), ())), preferred_element_type=F32)


def gram(table):
    return dot(table, table, ((0,), (0,)))


def model_part(rows, grams):
    high = grams.astype(BF16)
    low = (grams - high.astype(F32)).astype(BF16)
    return dot(rows, high) + dot(rows, low)


def take(ref, which, extent):
    return ref[pl.ds(pl.multiple_of(which * extent, extent), extent), :]


def pair_blocks(ref, freq_at, subj_at, n_freq):
    half_ta = ref.shape[0] // 2
    rank = ref.shape[2]
    freq = ref[pl.ds(freq_at * half_ta, half_ta), :n_freq, :]
    subj = ref[pl.ds(subj_at * half_ta, half_ta), n_freq:, :]
    return freq.reshape(-1, rank), subj.reshape(-1, rank)


def fetch_body(blocks_ref, got_ref, data_ref, grams_ref, time_ref, sems, wide, time_table):
    cap, bt, cells = data_ref.shape
    parts = sems.shape[1]
    rows = bt // parts
    copies = [
        pltpu.make_async_copy(
            blocks_ref.at[0, 0, 0, slot, pl.ds(part * rows, rows)],
            data_ref.at[slot, pl.ds(part * rows, rows)],
            sems.at[slot, part],
        )
        for slot in range(cap)
        for part in range(parts)
    ]
    for copy in copies:
        copy.start()
    slots = got_ref.shape[0]
    wide[...] = got_ref[...].astype(F32).reshape(slots * 8, HALF)
    for half in range(2):
        for row in range(ROWS):
            time_table[half, pl.ds(row, slots, stride=ROWS), :] = wide[
                pl.ds(2 * half + row, slots, stride=8), :
            ]
    time_ref[...] = jnp.concatenate([time_table[0], time_table[1]], axis=1).astype(BF16)
    for which in range(2):
        grams_ref[which] = gram(take(time_ref, which, time_ref.shape[0] // 2))
    for copy in copies:
        copy.wait()


def pair_body(
    n_freq,
    where_ref,
    data_ref,
    time_ref,
    time_grams_ref,
    second_ref,
    pair_ref,
    grams,
    freq,
    subj,
):
    n_ta = second_ref.shape[0]
    bf = freq.shape[0] // 2
    bs = subj.shape[0] // 2
    bt = time_ref.shape[0] // 2
    n_subj = second_ref.shape[1] - n_freq
    step = min(8, bf)
    cap = data_ref.shape[0]
    tables = []
    for slot in range(cap):
        a = take(time_ref, where_ref[0, slot], bt)
        tables.append((a, *pair_blocks(second_ref, where_ref[1, slot], where_ref[2, slot], n_freq)))

    def product(slot, j):
        cells = data_ref[slot, :, j * bs : (j + step) * bs]
        return dot(cells, tables[slot][0], ((0,), (0,))).reshape(step, bs, -1)

    chunks = [(slot, j) for slot in range(cap) for j in range(0, bf, step)]
    ahead = product(*chunks[0])
    freq[...] = jnp.zeros_like(freq)
    subj[...] = jnp.zeros_like(subj)
    for which in range(2):
        b, c = pair_blocks(second_ref, which, which, n_freq)
        grams[which] = gram(b)
        grams[2 + which] = gram(c)
    for at, (slot, j) in enumerate(chunks):
        cube = ahead
        if at + 1 < len(chunks):
            ahead = product(*chunks[at + 1])
        a, b, c = tables[slot]
        if j == 0:
            wide_b, wide_c = b.astype(F32), c.astype(F32)
            freq_data = []
            subj_data = jnp.zeros(wide_c.shape, F32)
        freq_data.append(jnp.sum(cube * wide_c[None], axis=1))
        for k in range(step):
            subj_data += cube[k] * wide_b[j + k : j + k + 1]
        if j + step == bf:
            live = slot < where_ref[3, slot]
            freq_at, subj_at = where_ref[1, slot], where_ref[2, slot]
            time_gram = time_grams_ref[where_ref[0, slot]]
            freq_grad = model_part(b, time_gram * grams[2 + subj_at])
            subj_grad = model_part(c, time_gram * grams[freq_at])
            freq_grad = jnp.where(live, freq_grad - jnp.concatenate(freq_data, axis=0), 0.0)
            subj_grad = jnp.where(live, subj_grad - subj_data, 0.0)
            freq[pl.ds(pl.multiple_of(freq_at * bf, bf), bf), :] += freq_grad
            subj[pl.ds(pl.multiple_of(subj_at * bs, bs), bs), :] += subj_grad

    for t in range(n_ta):
        pair_ref[t, :n_freq, :] = freq[t * n_freq : (t + 1) * n_freq, :].astype(SEND)
        pair_ref[t, n_freq:, :] = subj[t * n_subj : (t + 1) * n_subj, :].astype(SEND)


def time_body(n_freq, where_ref, data_ref, time_ref, second_ref, out_ref, grad):
    bt = data_ref.shape[1]
    grad[...] = jnp.zeros_like(grad)
    for slot in range(data_ref.shape[0]):
        live = slot < where_ref[3, slot]
        time_at = where_ref[0, slot]
        a = take(time_ref, time_at, bt)
        b, c = pair_blocks(second_ref, where_ref[1, slot], where_ref[2, slot], n_freq)
        bf, bs = b.shape[0], c.shape[0]
        step = min(8, bf)
        total = model_part(a, gram(b) * gram(c))
        for j in range(0, bf, step):
            khatri = (b[j : j + step][:, None, :] * c[None]).reshape(step * bs, -1)
            total -= dot(data_ref[slot, :, j * bs : (j + step) * bs], khatri)
        grad[pl.ds(pl.multiple_of(time_at * bt, bt), bt), :] += jnp.where(live, total, 0.0)

    for half in range(2):
        out_ref[half] = grad[:, half * HALF : (half + 1) * HALF]


def kernel_call(body, out_shape, in_spaces, scratch, name, cost, limit):
    return pl.pallas_call(
        body,
        out_shape=out_shape,
        in_specs=[pl.BlockSpec(memory_space=space) for space in in_spaces],
        out_specs=jax.tree.map(lambda _: pl.BlockSpec(memory_space=pltpu.VMEM), out_shape),
        scratch_shapes=scratch,
        compiler_params=pltpu.CompilerParams(vmem_limit_bytes=limit),
        cost_estimate=pl.CostEstimate(flops=cost, bytes_accessed=cost // 200, transcendentals=0),
        name=name,
    )


def fetch(blocks, first):
    cap, bt, cells = blocks.shape[3:]
    slots = first.shape[0]
    table, rank = ROWS * slots, 2 * HALF
    return kernel_call(
        fetch_body,
        [
            jax.ShapeDtypeStruct((cap, bt, cells), BF16),
            jax.ShapeDtypeStruct((2, rank, rank), F32),
            jax.ShapeDtypeStruct((table, rank), BF16),
        ],
        [pltpu.HBM, pltpu.VMEM],
        [
            pltpu.SemaphoreType.DMA((cap, 4)),
            pltpu.VMEM((slots * 8, HALF), F32),
            pltpu.VMEM((2, table, HALF), F32),
        ],
        "fetch",
        cap * bt * cells * 4,
        FETCH,
    )(blocks, first)


def pair_grads(n_freq, n_subj, slots_of, data, time_table, time_grams, second):
    n_ta, rows, rank = second.shape
    return kernel_call(
        functools.partial(pair_body, n_freq),
        jax.ShapeDtypeStruct(second.shape, SEND),
        [pltpu.SMEM] + [pltpu.VMEM] * 4,
        [
            pltpu.VMEM((4, rank, rank), F32),
            pltpu.VMEM((n_ta * n_freq, rank), F32),
            pltpu.VMEM((n_ta * n_subj, rank), F32),
        ],
        "pair_grads",
        2 * data.size * rank,
        BIG,
    )(slots_of, data, time_table, time_grams, second)


def time_grads(n_freq, slots_of, data, time_table, second):
    return kernel_call(
        functools.partial(time_body, n_freq),
        jax.ShapeDtypeStruct((2, time_table.shape[0], HALF), F32),
        [pltpu.SMEM] + [pltpu.VMEM] * 3,
        [pltpu.VMEM(time_table.shape, F32)],
        "time_grads",
        2 * data.size * time_table.shape[1],
        BIG,
    )(slots_of, data, time_table, second)


def pack_grads(n_af, n_sa, got_ref, time_ref, out_ref, own_ref, summed, wide):
    af = lax.axis_index("af")
    slots = n_af * n_sa
    n_freq = ROWS * n_sa
    total = jnp.sum(got_ref[...].astype(F32), axis=0)
    for half in range(2):
        summed[half] = total[:, half * HALF : (half + 1) * HALF]
    for half in range(2):
        for row in range(ROWS):
            wide[pl.ds(2 * half + row, slots, stride=8), :] = time_ref[
                half, pl.ds(row, slots, stride=ROWS), :
            ]
            at = 4 + 2 * half + row
            for peer in range(n_af):
                there = n_freq + ROWS * peer + row
                subj = summed[half, there : there + 1, :]
                wide[pl.ds(peer * n_sa * 8 + at, n_sa, stride=8), :] = jnp.broadcast_to(
                    subj, (n_sa, HALF)
                )
            wide[pl.ds(af * (n_sa * 8) + at, n_sa, stride=8), :] = summed[
                half, pl.ds(row, n_sa, stride=ROWS), :
            ]
        own_ref[:, half * HALF : (half + 1) * HALF] = summed[
            half, pl.ds(n_freq + ROWS * af, ROWS), :
        ]
    out_ref[...] = wide[...].astype(SEND).reshape(slots, 8, HALF)


def update(
    n_af,
    n_sa,
    got_ref,
    own_ref,
    time_ref,
    freq_ref,
    subj_ref,
    time_vel_ref,
    freq_vel_ref,
    subj_vel_ref,
    new_time_ref,
    new_freq_ref,
    new_subj_ref,
    new_time_vel_ref,
    new_freq_vel_ref,
    new_subj_vel_ref,
):
    af = lax.axis_index("af")
    sa = lax.axis_index("sa")
    time = jnp.sum(got_ref[...].astype(F32), axis=0)
    freq = jnp.sum(got_ref[pl.ds(af * n_sa, n_sa)].astype(F32), axis=0)
    subj = jnp.zeros_like(freq)
    for peer in range(n_af):
        there = got_ref[peer * n_sa + sa].astype(F32)
        subj += jnp.where(peer == af, jnp.zeros_like(there), there)
    own = own_ref[...]
    for half in range(2):
        lanes = slice(half * HALF, (half + 1) * HALF)
        rows = slice(2 * half, 2 * half + 2)
        more = slice(4 + 2 * half, 6 + 2 * half)
        for grad, old, vel, new, new_vel in (
            (time[rows], time_ref, time_vel_ref, new_time_ref, new_time_vel_ref),
            (freq[more], freq_ref, freq_vel_ref, new_freq_ref, new_freq_vel_ref),
            (subj[more] + own[:, lanes], subj_ref, subj_vel_ref, new_subj_ref, new_subj_vel_ref),
        ):
            velocity = 0.9 * vel[0, :, lanes] + grad / 64.0
            new_vel[0, :, lanes] = velocity
            new[0, :, lanes] = old[0, :, lanes] - 0.5 * velocity


def per_device(sizes, *args):
    n_ta, n_af, n_sa = sizes
    blocks, coords, counts, time, freq, subj, time_vel, freq_vel, subj_vel = args
    slots = n_af * n_sa
    rank = time.shape[-1]
    pair_rows = ROWS * (n_sa + n_af)
    coords = coords.transpose(0, 1, 2, 4, 3).reshape(3, -1)
    slots_of = jnp.concatenate([coords, jnp.broadcast_to(counts.reshape(1, 1), (1, coords.shape[1]))])

    packed = pl.pallas_call(
        functools.partial(pack_factors, n_sa),
        out_shape=jax.ShapeDtypeStruct((slots, 8, HALF), BF16),
        scratch_shapes=[pltpu.VMEM((8, HALF), F32)] * 2,
        compiler_params=pltpu.CompilerParams(vmem_limit_bytes=SMALL),
        name="pack_factors",
    )(jnp.concatenate([time, freq, subj], axis=0))
    first = lax.all_to_all(packed, ("af", "sa"), 0, 0, tiled=True)
    joined = pl.pallas_call(
        functools.partial(join_factors, n_af, n_sa),
        out_shape=jax.ShapeDtypeStruct((n_ta, pair_rows, rank), BF16),
        in_specs=[pl.BlockSpec(memory_space=pltpu.VMEM)] * 2,
        out_specs=pl.BlockSpec(memory_space=pltpu.HBM),
        scratch_shapes=[
            pltpu.VMEM((slots * 8, HALF), F32),
            pltpu.VMEM((2, pair_rows, HALF), F32),
            pltpu.VMEM((pair_rows, rank), BF16),
            pltpu.SemaphoreType.DMA((n_ta,)),
        ],
        compiler_params=pltpu.CompilerParams(vmem_limit_bytes=SMALL),
        name="join_factors",
    )(first, packed)
    second = lax.all_to_all(joined, "ta", 0, 0, tiled=True)
    data, time_grams, time_table = fetch(blocks, first)
    n_freq, n_subj = ROWS * n_sa, ROWS * n_af
    pair = pair_grads(n_freq, n_subj, slots_of, data, time_table, time_grams, second)
    time_grad = time_grads(n_freq, slots_of, data, time_table, second)
    third = lax.all_to_all(pair, "ta", 0, 0, tiled=True)
    packed_grads, own = pl.pallas_call(
        functools.partial(pack_grads, n_af, n_sa),
        out_shape=[
            jax.ShapeDtypeStruct((slots, 8, HALF), SEND),
            jax.ShapeDtypeStruct((ROWS, rank), F32),
        ],
        scratch_shapes=[
            pltpu.VMEM((2, pair_rows, HALF), F32),
            pltpu.VMEM((slots * 8, HALF), F32),
        ],
        compiler_params=pltpu.CompilerParams(vmem_limit_bytes=SMALL),
        name="pack_grads",
    )(third, time_grad)
    fourth = lax.all_to_all(packed_grads, ("af", "sa"), 0, 0, tiled=True)
    return pl.pallas_call(
        functools.partial(update, n_af, n_sa),
        out_shape=[jax.ShapeDtypeStruct(time.shape, F32)] * 6,
        compiler_params=pltpu.CompilerParams(vmem_limit_bytes=SMALL),
        name="update",
    )(fourth, own, time, freq, subj, time_vel, freq_vel, subj_vel)


def solution(mesh):
    sizes = tuple(mesh.shape[name] for name in ("ta", "af", "sa"))
    factors = (P("ta", ("af", "sa"), None), P("af", ("ta", "sa"), None), P("sa", ("ta", "af"), None))
    return jax.shard_map(
        lambda *args: tuple(per_device(sizes, *args)),
        mesh=mesh,
        in_specs=(
            P("ta", "af", "sa", None, None, None),
            P("ta", "af", "sa", None, None),
            P("ta", "af", "sa"),
            *factors,
            *factors,
        ),
        out_specs=(*factors, *factors),
        check_vma=False,
    )
```

```python
import functools

import jax
import jax.numpy as jnp
from jax import lax
from jax.experimental import pallas as pl
from jax.experimental.pallas import tpu as pltpu
from jax.sharding import PartitionSpec as P

BF16 = jnp.bfloat16
F32 = jnp.float32
ROWS = 2
HALF = 128
BIG = 24 << 20
FETCH = 53 * 1000 * 1000
SMALL = 4 << 20
SEND = BF16


def put_rows(tile, at, rows):
    tile[at : at + 2, :] = rows[:, :HALF]
    tile[at + 2 : at + 4, :] = rows[:, HALF:]


def pack_factors(n_sa, own_ref, out_ref, with_freq, with_subj):
    mine = lax.axis_index("af")
    put_rows(with_freq, 0, own_ref[0])
    put_rows(with_subj, 0, own_ref[0])
    put_rows(with_freq, 4, own_ref[1])
    put_rows(with_subj, 4, own_ref[2])
    freq_tile = with_freq[...].astype(BF16)
    subj_tile = with_subj[...].astype(BF16)
    out_ref[...] = jnp.broadcast_to(subj_tile[None], out_ref.shape)
    out_ref[pl.ds(mine * n_sa, n_sa)] = jnp.broadcast_to(freq_tile[None], (n_sa, 8, HALF))


def join_factors(n_af, n_sa, got_ref, packed_ref, out_ref, wide, joined):
    af = lax.axis_index("af")
    sa = lax.axis_index("sa")
    slots = n_af * n_sa
    wide[...] = got_ref[...].astype(F32).reshape(slots * 8, HALF)
    own = packed_ref[jnp.where(af == 0, n_sa, 0)].astype(F32)
    is_own = lax.broadcasted_iota(jnp.int32, (n_af, HALF), 0) == af
    for half in range(2):
        for row in range(ROWS):
            at = 4 + 2 * half + row
            freq = wide[pl.ds(af * (n_sa * 8) + at, n_sa, stride=8), :]
            joined[half, pl.ds(row, n_sa, stride=ROWS), :] = freq
            subj = wide[pl.ds(sa * 8 + at, n_af, stride=n_sa * 8), :]
            subj = jnp.where(is_own, own[at : at + 1], subj)
            joined[half, pl.ds(ROWS * n_sa + row, n_af, stride=ROWS), :] = subj
    rows = jnp.concatenate([joined[0], joined[1]], axis=1).astype(BF16)
    for peer in range(out_ref.shape[0]):
        out_ref[peer] = rows


def dot(a, b, contract=((1,), (0,))):
    return lax.dot_general(a, b, (contract, ((), ())), preferred_element_type=F32)


def gram(table):
    return dot(table, table, ((0,), (0,)))


def model_part(rows, grams):
    high = grams.astype(BF16)
    low = (grams - high.astype(F32)).astype(BF16)
    return dot(rows, high) + dot(rows, low)


def take(ref, which, extent):
    return ref[pl.ds(pl.multiple_of(which * extent, extent), extent), :]


def pair_blocks(ref, freq_at, subj_at, n_freq):
    half_ta = ref.shape[0] // 2
    rank = ref.shape[2]
    freq = ref[pl.ds(freq_at * half_ta, half_ta), :n_freq, :]
    subj = ref[pl.ds(subj_at * half_ta, half_ta), n_freq:, :]
    return freq.reshape(-1, rank), subj.reshape(-1, rank)


def fetch_body(blocks_ref, got_ref, data_ref, grams_ref, time_ref, sems, wide, time_table):
    cap, bt, cells = data_ref.shape
    parts = sems.shape[1]
    rows = bt // parts
    copies = [
        pltpu.make_async_copy(
            blocks_ref.at[0, 0, 0, slot, pl.ds(part * rows, rows)],
            data_ref.at[slot, pl.ds(part * rows, rows)],
            sems.at[slot, part],
        )
        for slot in range(cap)
        for part in range(parts)
    ]
    for copy in copies:
        copy.start()
    slots = got_ref.shape[0]
    wide[...] = got_ref[...].astype(F32).reshape(slots * 8, HALF)
    for half in range(2):
        for row in range(ROWS):
            time_table[half, pl.ds(row, slots, stride=ROWS), :] = wide[
                pl.ds(2 * half + row, slots, stride=8), :
            ]
    time_ref[...] = jnp.concatenate([time_table[0], time_table[1]], axis=1).astype(BF16)
    for which in range(2):
        grams_ref[which] = gram(take(time_ref, which, time_ref.shape[0] // 2))
    for copy in copies:
        copy.wait()


def pair_body(
    n_freq,
    where_ref,
    data_ref,
    time_ref,
    time_grams_ref,
    second_ref,
    pair_ref,
    grams,
    freq,
    subj,
):
    n_ta = second_ref.shape[0]
    bf = freq.shape[0] // 2
    bs = subj.shape[0] // 2
    bt = time_ref.shape[0] // 2
    n_subj = second_ref.shape[1] - n_freq
    freq[...] = jnp.zeros_like(freq)
    subj[...] = jnp.zeros_like(subj)
    for which in range(2):
        b, c = pair_blocks(second_ref, which, which, n_freq)
        grams[which] = gram(b)
        grams[2 + which] = gram(c)
    step = min(2, bf)
    cap = data_ref.shape[0]
    tables = []
    for slot in range(cap):
        a = take(time_ref, where_ref[0, slot], bt)
        tables.append((a, *pair_blocks(second_ref, where_ref[1, slot], where_ref[2, slot], n_freq)))

    def product(slot, j):
        cells = data_ref[slot, :, j * bs : (j + step) * bs]
        return dot(cells, tables[slot][0], ((0,), (0,))).reshape(step, bs, -1)

    chunks = [(slot, j) for slot in range(cap) for j in range(0, bf, step)]
    ahead = product(*chunks[0])
    for at, (slot, j) in enumerate(chunks):
        cube = ahead
        if at + 1 < len(chunks):
            ahead = product(*chunks[at + 1])
        a, b, c = tables[slot]
        if j == 0:
            wide_b, wide_c = b.astype(F32), c.astype(F32)
            freq_data = []
            subj_data = jnp.zeros(wide_c.shape, F32)
        for k in range(step):
            freq_data.append(jnp.sum((cube[k] * wide_c).reshape(bs // 8, 8, -1), axis=0))
            subj_data += cube[k] * wide_b[j + k : j + k + 1]
        if j + step == bf:
            live = slot < where_ref[3, slot]
            freq_at, subj_at = where_ref[1, slot], where_ref[2, slot]
            time_gram = time_grams_ref[where_ref[0, slot]]
            freq_grad = model_part(b, time_gram * grams[2 + subj_at])
            subj_grad = model_part(c, time_gram * grams[freq_at])
            freq_data = [
                jnp.sum(jnp.stack(freq_data[row : row + 8]), axis=1) for row in range(0, bf, 8)
            ]
            freq_grad = jnp.where(live, freq_grad - jnp.concatenate(freq_data, axis=0), 0.0)
            subj_grad = jnp.where(live, subj_grad - subj_data, 0.0)
            freq[pl.ds(pl.multiple_of(freq_at * bf, bf), bf), :] += freq_grad
            subj[pl.ds(pl.multiple_of(subj_at * bs, bs), bs), :] += subj_grad

    for t in range(n_ta):
        pair_ref[t, :n_freq, :] = freq[t * n_freq : (t + 1) * n_freq, :].astype(SEND)
        pair_ref[t, n_freq:, :] = subj[t * n_subj : (t + 1) * n_subj, :].astype(SEND)


def time_body(n_freq, where_ref, data_ref, time_ref, second_ref, out_ref, grad):
    bt = data_ref.shape[1]
    grad[...] = jnp.zeros_like(grad)
    for slot in range(data_ref.shape[0]):
        live = slot < where_ref[3, slot]
        time_at = where_ref[0, slot]
        a = take(time_ref, time_at, bt)
        b, c = pair_blocks(second_ref, where_ref[1, slot], where_ref[2, slot], n_freq)
        bf, bs = b.shape[0], c.shape[0]
        step = min(8, bf)
        total = model_part(a, gram(b) * gram(c))
        for j in range(0, bf, step):
            khatri = (b[j : j + step][:, None, :] * c[None]).reshape(step * bs, -1)
            total -= dot(data_ref[slot, :, j * bs : (j + step) * bs], khatri)
        grad[pl.ds(pl.multiple_of(time_at * bt, bt), bt), :] += jnp.where(live, total, 0.0)

    for half in range(2):
        out_ref[half] = grad[:, half * HALF : (half + 1) * HALF]


def kernel_call(body, out_shape, in_spaces, scratch, name, cost, limit):
    return pl.pallas_call(
        body,
        out_shape=out_shape,
        in_specs=[pl.BlockSpec(memory_space=space) for space in in_spaces],
        out_specs=jax.tree.map(lambda _: pl.BlockSpec(memory_space=pltpu.VMEM), out_shape),
        scratch_shapes=scratch,
        compiler_params=pltpu.CompilerParams(vmem_limit_bytes=limit),
        cost_estimate=pl.CostEstimate(flops=cost, bytes_accessed=cost // 200, transcendentals=0),
        name=name,
    )


def fetch(blocks, first):
    cap, bt, cells = blocks.shape[3:]
    slots = first.shape[0]
    table, rank = ROWS * slots, 2 * HALF
    return kernel_call(
        fetch_body,
        [
            jax.ShapeDtypeStruct((cap, bt, cells), BF16),
            jax.ShapeDtypeStruct((2, rank, rank), F32),
            jax.ShapeDtypeStruct((table, rank), BF16),
        ],
        [pltpu.HBM, pltpu.VMEM],
        [
            pltpu.SemaphoreType.DMA((cap, 4)),
            pltpu.VMEM((slots * 8, HALF), F32),
            pltpu.VMEM((2, table, HALF), F32),
        ],
        "fetch",
        cap * bt * cells * 4,
        FETCH,
    )(blocks, first)


def pair_grads(n_freq, n_subj, slots_of, data, time_table, time_grams, second):
    n_ta, rows, rank = second.shape
    return kernel_call(
        functools.partial(pair_body, n_freq),
        jax.ShapeDtypeStruct(second.shape, SEND),
        [pltpu.SMEM] + [pltpu.VMEM] * 4,
        [
            pltpu.VMEM((4, rank, rank), F32),
            pltpu.VMEM((n_ta * n_freq, rank), F32),
            pltpu.VMEM((n_ta * n_subj, rank), F32),
        ],
        "pair_grads",
        2 * data.size * rank,
        BIG,
    )(slots_of, data, time_table, time_grams, second)


def time_grads(n_freq, slots_of, data, time_table, second):
    return kernel_call(
        functools.partial(time_body, n_freq),
        jax.ShapeDtypeStruct((2, time_table.shape[0], HALF), F32),
        [pltpu.SMEM] + [pltpu.VMEM] * 3,
        [pltpu.VMEM(time_table.shape, F32)],
        "time_grads",
        2 * data.size * time_table.shape[1],
        BIG,
    )(slots_of, data, time_table, second)


def pack_grads(n_af, n_sa, got_ref, time_ref, out_ref, own_ref, summed, wide):
    af = lax.axis_index("af")
    slots = n_af * n_sa
    n_freq = ROWS * n_sa
    total = jnp.sum(got_ref[...].astype(F32), axis=0)
    for half in range(2):
        summed[half] = total[:, half * HALF : (half + 1) * HALF]
    for half in range(2):
        for row in range(ROWS):
            wide[pl.ds(2 * half + row, slots, stride=8), :] = time_ref[
                half, pl.ds(row, slots, stride=ROWS), :
            ]
            at = 4 + 2 * half + row
            for peer in range(n_af):
                there = n_freq + ROWS * peer + row
                subj = summed[half, there : there + 1, :]
                wide[pl.ds(peer * n_sa * 8 + at, n_sa, stride=8), :] = jnp.broadcast_to(
                    subj, (n_sa, HALF)
                )
            wide[pl.ds(af * (n_sa * 8) + at, n_sa, stride=8), :] = summed[
                half, pl.ds(row, n_sa, stride=ROWS), :
            ]
        own_ref[:, half * HALF : (half + 1) * HALF] = summed[
            half, pl.ds(n_freq + ROWS * af, ROWS), :
        ]
    out_ref[...] = wide[...].astype(SEND).reshape(slots, 8, HALF)


def update(
    n_af,
    n_sa,
    got_ref,
    own_ref,
    time_ref,
    freq_ref,
    subj_ref,
    time_vel_ref,
    freq_vel_ref,
    subj_vel_ref,
    new_time_ref,
    new_freq_ref,
    new_subj_ref,
    new_time_vel_ref,
    new_freq_vel_ref,
    new_subj_vel_ref,
):
    af = lax.axis_index("af")
    sa = lax.axis_index("sa")
    time = jnp.sum(got_ref[...].astype(F32), axis=0)
    freq = jnp.sum(got_ref[pl.ds(af * n_sa, n_sa)].astype(F32), axis=0)
    subj = jnp.zeros_like(freq)
    for peer in range(n_af):
        there = got_ref[peer * n_sa + sa].astype(F32)
        subj += jnp.where(peer == af, jnp.zeros_like(there), there)
    own = own_ref[...]
    for half in range(2):
        lanes = slice(half * HALF, (half + 1) * HALF)
        rows = slice(2 * half, 2 * half + 2)
        more = slice(4 + 2 * half, 6 + 2 * half)
        for grad, old, vel, new, new_vel in (
            (time[rows], time_ref, time_vel_ref, new_time_ref, new_time_vel_ref),
            (freq[more], freq_ref, freq_vel_ref, new_freq_ref, new_freq_vel_ref),
            (subj[more] + own[:, lanes], subj_ref, subj_vel_ref, new_subj_ref, new_subj_vel_ref),
        ):
            velocity = 0.9 * vel[0, :, lanes] + grad / 64.0
            new_vel[0, :, lanes] = velocity
            new[0, :, lanes] = old[0, :, lanes] - 0.5 * velocity


def per_device(sizes, *args):
    n_ta, n_af, n_sa = sizes
    blocks, coords, counts, time, freq, subj, time_vel, freq_vel, subj_vel = args
    slots = n_af * n_sa
    rank = time.shape[-1]
    pair_rows = ROWS * (n_sa + n_af)
    coords = coords.transpose(0, 1, 2, 4, 3).reshape(3, -1)
    slots_of = jnp.concatenate([coords, jnp.broadcast_to(counts.reshape(1, 1), (1, coords.shape[1]))])

    packed = pl.pallas_call(
        functools.partial(pack_factors, n_sa),
        out_shape=jax.ShapeDtypeStruct((slots, 8, HALF), BF16),
        scratch_shapes=[pltpu.VMEM((8, HALF), F32)] * 2,
        compiler_params=pltpu.CompilerParams(vmem_limit_bytes=SMALL),
        name="pack_factors",
    )(jnp.concatenate([time, freq, subj], axis=0))
    first = lax.all_to_all(packed, ("af", "sa"), 0, 0, tiled=True)
    joined = pl.pallas_call(
        functools.partial(join_factors, n_af, n_sa),
        out_shape=jax.ShapeDtypeStruct((n_ta, pair_rows, rank), BF16),
        scratch_shapes=[
            pltpu.VMEM((slots * 8, HALF), F32),
            pltpu.VMEM((2, pair_rows, HALF), F32),
        ],
        compiler_params=pltpu.CompilerParams(vmem_limit_bytes=SMALL),
        name="join_factors",
    )(first, packed)
    second = lax.all_to_all(joined, "ta", 0, 0, tiled=True)
    data, time_grams, time_table = fetch(blocks, first)
    n_freq, n_subj = ROWS * n_sa, ROWS * n_af
    pair = pair_grads(n_freq, n_subj, slots_of, data, time_table, time_grams, second)
    time_grad = time_grads(n_freq, slots_of, data, time_table, second)
    third = lax.all_to_all(pair, "ta", 0, 0, tiled=True)
    packed_grads, own = pl.pallas_call(
        functools.partial(pack_grads, n_af, n_sa),
        out_shape=[
            jax.ShapeDtypeStruct((slots, 8, HALF), SEND),
            jax.ShapeDtypeStruct((ROWS, rank), F32),
        ],
        scratch_shapes=[
            pltpu.VMEM((2, pair_rows, HALF), F32),
            pltpu.VMEM((slots * 8, HALF), F32),
        ],
        compiler_params=pltpu.CompilerParams(vmem_limit_bytes=SMALL),
        name="pack_grads",
    )(third, time_grad)
    fourth = lax.all_to_all(packed_grads, ("af", "sa"), 0, 0, tiled=True)
    return pl.pallas_call(
        functools.partial(update, n_af, n_sa),
        out_shape=[jax.ShapeDtypeStruct(time.shape, F32)] * 6,
        compiler_params=pltpu.CompilerParams(vmem_limit_bytes=SMALL),
        name="update",
    )(fourth, own, time, freq, subj, time_vel, freq_vel, subj_vel)


def solution(mesh):
    sizes = tuple(mesh.shape[name] for name in ("ta", "af", "sa"))
    factors = (P("ta", ("af", "sa"), None), P("af", ("ta", "sa"), None), P("sa", ("ta", "af"), None))
    return jax.shard_map(
        lambda *args: tuple(per_device(sizes, *args)),
        mesh=mesh,
        in_specs=(
            P("ta", "af", "sa", None, None, None),
            P("ta", "af", "sa", None, None),
            P("ta", "af", "sa"),
            *factors,
            *factors,
        ),
        out_specs=(*factors, *factors),
        check_vma=False,
    )
```
